32 devices in a mesh: dp: 16 (over z, y, x), ctx: 2 (over core).
Axes of the slice: x: 2, y: 2, z: 4, core: 2. Of those that a mesh axis runs over, the one named last changes fastest.
Arguments:
- features: bfloat16 [16, 256, 2048], P('dp', 'ctx'), may hold values from -6 to 6
- log_decays: float32 [16, 256, 32], P('dp', 'ctx'), may hold values from -0.9 to 0, as said below
- cotangent: bfloat16 [16, 256, 2048], P('dp', 'ctx'), may hold values from -6 to 6
- bc_weight: bfloat16 [2048, 256], P('ctx'), may hold values from -0.125 to 0.125
Outputs:
- grad_features: bfloat16 [16, 256, 2048], P('dp', 'ctx')
- grad_weight: bfloat16 [2048, 256], P('ctx')
The draws below stay inside these ranges and needn't reach their ends.
Inputs may be any that keep to these rules, and one draw needn't show every extreme that they name: log_decays holds the logarithm of each position's and head's decay factor.
All inputs are finite; a program needn't handle non-finite values.
Results may differ from the reference program's by a relative error of at most 0.0075.
Values may be sent and summed in bfloat16 or wider, within the bound.
A program may use at most 64 MiB of HBM per device.

```python
import math
import jax
import jax.numpy as jnp
from jax import lax

HEADS = 32
STATE = 128
BLOCK = 128
L_DEV = 128
WIDTH = 2048
STRAND_TOTAL = 16
BASES_PER_READ = 256


def draw_log_decays(key, part):
    derived_prng_keys = jax.random.split(key, 7)
    shape_heads = (STRAND_TOTAL, 1, HEADS)
    slow_share = 0.5
    chosen = jax.random.uniform(derived_prng_keys[0], shape_heads)
    slow_time = jnp.exp(jax.random.uniform(derived_prng_keys[1], shape_heads, minval=math.log(BASES_PER_READ), maxval=math.log(8 * BASES_PER_READ)))
    fast_time = jnp.exp(jax.random.uniform(derived_prng_keys[2], shape_heads, minval=math.log(20.0), maxval=math.log(60.0)))
    fading_speeds = jnp.where(chosen < slow_share, 1.0 / slow_time, 1.0 / fast_time)
    gaussian_jitter = jax.random.uniform(derived_prng_keys[3], (STRAND_TOTAL, BASES_PER_READ, HEADS), minval=0.5, maxval=1.5)
    blocks = BASES_PER_READ // L_DEV
    speed_interval = jnp.exp(jax.random.uniform(derived_prng_keys[4], (STRAND_TOTAL, blocks, 1, HEADS), minval=-0.7, maxval=0.7))
    speed_interval = jnp.broadcast_to(speed_interval, (STRAND_TOTAL, blocks, L_DEV, HEADS)).reshape(STRAND_TOTAL, BASES_PER_READ, HEADS)
    jump_occurrences = jax.random.uniform(derived_prng_keys[5], (STRAND_TOTAL, BASES_PER_READ, 1)) < 3.0 / BASES_PER_READ
    jump_reduction = jnp.log(jax.random.uniform(derived_prng_keys[6], (STRAND_TOTAL, BASES_PER_READ, 1), minval=0.5, maxval=0.8))
    layer_response = -fading_speeds * gaussian_jitter * speed_interval + jnp.where(jump_occurrences, jump_reduction, 0.0)
    return layer_response.astype(jnp.float32)


def block_levels(stream_key, extent, cuts, low, largest):
    def one(position, parts):
        steps = jax.random.uniform(jax.random.fold_in(jax.random.fold_in(stream_key, 6), position), (parts,), jnp.float32, low / len(cuts), largest / len(cuts))
        return jnp.repeat(jnp.exp(steps), extent[position] // parts).reshape((-1,) + (1,) * (len(extent) - position - 1))

    gain = one(*cuts[0])
    for cut in cuts[1:]:
        gain = gain * one(*cut)
    return gain


def scatter_about(stream_key, shape, spread, bound, cuts=(), held_as=jnp.bfloat16):
    result = spread * jax.random.normal(stream_key, shape, jnp.float32)
    if cuts:
        result = result * block_levels(stream_key, shape, cuts, -0.22, 0.18)
    return jnp.clip(result, -bound, bound).astype(held_as)


def setup_inputs(seed: int = 0) -> dict:
    key_list = jax.random.split(jax.random.key(seed), 5)
    features = scatter_about(key_list[0], (STRAND_TOTAL, BASES_PER_READ, WIDTH), 1.0, 6.0, ((0, 16), (1, 2)))
    log_decays = draw_log_decays(jax.random.fold_in(key_list[4], 71), 0)
    cotangent = scatter_about(key_list[2], (STRAND_TOTAL, BASES_PER_READ, WIDTH), 1.0, 6.0, ((0, 16), (1, 2)))
    bc_weight = scatter_about(key_list[3], (WIDTH, 2 * STATE), WIDTH ** -0.5, 0.125, ((0, 2),))
    return {"features": features, "log_decays": log_decays, "cotangent": cotangent, "bc_weight": bc_weight}


def core(tokens, log_rates, cotangent, bc_vals, head_count, block, linking):
    row_count, feat_width = tokens.shape
    head_dim = feat_width // head_count
    state_size = bc_vals.shape[1] // 2
    block_count = row_count // block
    inv_root = state_size ** (-0.5)
    highest = lax.Precision.HIGHEST
    b_in = bc_vals[:, :state_size].astype(jnp.float32).reshape(block_count, block, state_size)
    c_out = bc_vals[:, state_size:].astype(jnp.float32).reshape(block_count, block, state_size)
    x_full = tokens.astype(jnp.float32).reshape(block_count, block, head_count, head_dim)
    g_full = cotangent.astype(jnp.float32).reshape(block_count, block, head_count, head_dim)
    log_rate = log_rates.reshape(block_count, block, head_count)
    inclusive = jnp.cumsum(log_rate, axis=1)
    exclusive = inclusive - log_rate
    block_sum = inclusive[:, -1, :]
    step_size = jnp.sqrt(-jnp.expm1(2.0 * log_rate))
    tail_rate = jnp.exp(block_sum[:, None, :] - inclusive)
    head_rate = jnp.exp(exclusive)
    tail_excl = jnp.exp(block_sum[:, None, :] - exclusive)
    head_incl = jnp.exp(inclusive)

    def summary(values, weights, basis):
        return jnp.einsum('kthp,ktn->khpn', values * weights[..., None], basis, precision=highest)
    h_loc = summary(x_full, tail_rate * step_size, b_in)
    r_loc = summary(x_full, head_rate * step_size, b_in)
    rho_loc = summary(g_full, tail_excl * inv_root, c_out)
    lam_loc = summary(g_full, head_incl * inv_root, c_out)
    z_incl = jnp.cumsum(block_sum, axis=0)
    z_excl = z_incl - block_sum
    z_last = z_incl[-1]
    block_pos = jnp.arange(block_count)
    before = (block_pos[:, None] > block_pos[None, :])[:, :, None]
    after_mask = (block_pos[:, None] < block_pos[None, :])[:, :, None]
    up_mat = jnp.where(before, jnp.exp(jnp.where(before, z_excl[:, None, :] - z_incl[None, :, :], 0.0)), 0.0)
    dn_mat = jnp.where(after_mask, jnp.exp(jnp.where(after_mask, z_excl[None, :, :] - z_incl[:, None, :], 0.0)), 0.0)
    to_end = jnp.exp(z_last[None, :] - z_incl)
    from_start = jnp.exp(z_excl)

    def speed_interval(matrix, summaries):
        return jnp.einsum('kjh,jhpn->khpn', matrix, summaries, precision=highest)

    def fold(weights, summaries):
        return jnp.einsum('jh,jhpn->hpn', weights, summaries, precision=highest)
    up_dev = (fold(to_end, h_loc), fold(to_end, rho_loc))
    dn_dev = (fold(from_start, r_loc), fold(from_start, lam_loc))
    up_in, dn_in = linking(jnp.exp(z_last), up_dev, dn_dev)
    h_in = speed_interval(up_mat, h_loc) + from_start[:, :, None, None] * up_in[0][None]
    rho_in = speed_interval(up_mat, rho_loc) + from_start[:, :, None, None] * up_in[1][None]
    r_in = speed_interval(dn_mat, r_loc) + to_end[:, :, None, None] * dn_in[0][None]
    lam_in = speed_interval(dn_mat, lam_loc) + to_end[:, :, None, None] * dn_in[1][None]
    positions = jnp.arange(block)
    lower_mask = positions[:, None] >= positions[None, :]
    upper_mask = positions[:, None] <= positions[None, :]
    incl_h = jnp.swapaxes(inclusive, 1, 2)
    excl_h = jnp.swapaxes(exclusive, 1, 2)
    step_h = jnp.swapaxes(step_size, 1, 2)
    forward_w = jnp.where(lower_mask, jnp.exp(jnp.where(lower_mask, incl_h[:, :, :, None] - incl_h[:, :, None, :], 0.0)), 0.0)
    backward_w = jnp.where(upper_mask, jnp.exp(jnp.where(upper_mask, excl_h[:, :, None, :] - excl_h[:, :, :, None], 0.0)), 0.0)
    mix_weight = forward_w + backward_w
    cross_dot = jnp.einsum('ktbp,ksbp->kbts', g_full, x_full, precision=highest)
    weight_c = lax.optimization_barrier(jnp.sum(mix_weight * cross_dot * step_h[:, :, None, :], axis=1))
    weight_b = jnp.swapaxes(weight_c, 1, 2)
    grad_c = jnp.einsum('kts,ksn->ktn', weight_c, b_in, precision=highest)
    grad_c = grad_c + jnp.einsum('kthp,khpn->ktn', g_full * head_incl[..., None], h_in, precision=highest)
    grad_c = inv_root * (grad_c + jnp.einsum('kthp,khpn->ktn', g_full * tail_excl[..., None], r_in, precision=highest))
    grad_b = inv_root * jnp.einsum('kts,ksn->ktn', weight_b, c_out, precision=highest)
    grad_b = grad_b + jnp.einsum('kthp,khpn->ktn', x_full * (step_size * tail_rate)[..., None], lam_in, precision=highest)
    grad_b = grad_b + jnp.einsum('kthp,khpn->ktn', x_full * (step_size * head_rate)[..., None], rho_in, precision=highest)
    intersection = jnp.einsum('ktn,ksn->kts', c_out, b_in, precision=highest)
    pair_weight = jnp.swapaxes(mix_weight, 2, 3) * jnp.swapaxes(intersection, 1, 2)[:, None]
    inner = inv_root * jnp.einsum('khts,kshp->kthp', pair_weight, g_full, precision=highest)
    inner = inner + jnp.einsum('khpn,ktn->kthp', lam_in, b_in, precision=highest) * tail_rate[..., None]
    inner = inner + jnp.einsum('khpn,ktn->kthp', rho_in, b_in, precision=highest) * head_rate[..., None]
    grad_x = (inner * step_size[..., None]).reshape(row_count, feat_width)
    grad_bc = jnp.concatenate([grad_b, grad_c], axis=-1).reshape(row_count, 2 * state_size).astype(jnp.bfloat16)
    return (grad_x, grad_bc)

def no_links(decay, up_dev, dn_dev):
    return ((jnp.zeros_like(up_dev[0]), jnp.zeros_like(up_dev[1])), (jnp.zeros_like(dn_dev[0]), jnp.zeros_like(dn_dev[1])))

def reference(features, log_decays, cotangent, bc_weight):
    head_count = log_decays.shape[2]

    def per_sequence(inputs):
        tokens, log_rates, grads = inputs
        bc_vals = jnp.dot(tokens, bc_weight, preferred_element_type=jnp.float32).astype(jnp.bfloat16)
        grad_x, grad_bc = core(tokens, log_rates, grads, bc_vals, head_count, BLOCK, no_links)
        back_proj = jnp.dot(grad_bc, bc_weight.T, preferred_element_type=jnp.float32)
        grad_tokens = (grad_x + back_proj).astype(jnp.bfloat16)
        grad_local = jnp.dot(tokens.T, grad_bc, preferred_element_type=jnp.float32)
        return (grad_tokens, grad_local)
    grad_tokens, grad_local = lax.map(per_sequence, (features, log_decays, cotangent))
    grad_weight = (lax.optimization_barrier(jnp.sum(grad_local, axis=0)) * (STRAND_TOTAL * BASES_PER_READ) ** (-0.5)).astype(jnp.bfloat16)
    return (grad_tokens, grad_weight)
```

```python
import functools

import jax
import jax.numpy as jnp
from jax import lax
from jax.experimental import pallas as pl
from jax.experimental.pallas import tpu as pltpu
from jax.sharding import PartitionSpec as P

MESH = pl.DeviceIdType.MESH
F32 = jnp.float32
BF16 = jnp.bfloat16
NN = (((1,), (0,)), ((), ()))
NT = (((1,), (1,)), ((), ()))
QUAD = 4


def mm(a, b, dims=NN):
    return lax.dot_general(a, b, dims, preferred_element_type=F32)


def flip(a):
    return jnp.transpose(a.astype(F32)).astype(a.dtype)


def one_minus_exp(y):
    z = y * 0.125
    f = z * (1.0 + z * (1 / 2) * (1.0 + z * (1 / 3) * (1.0 + z * (1 / 4) * (1.0 + z * (1 / 5) * (1.0 + z * (1 / 6) * (1.0 + z * (1 / 7)))))))
    for _ in range(3):
        f = f * (f + 2.0)
    return -f


def rotate(place, by, count):
    return lax.rem(place + by, count)


def body(line, total_rows, head_count, x_hbm, lr_hbm, g_hbm, w_hbm, gf_ref, gw_ref,
         x_ref, lr_ref, g_ref, w_ref, w_other, xt, xr, xs, xw, gs, s_send, s_recv, gx, bc_all,
         acc, half_send, half_recv, z_send, z_recv,
         in_sem, w_sem, s_sem_s, s_sem_r, x_sem_s, x_sem_r, b_sem_s, b_sem_r, h_sem,
         z_sem_s, z_sem_r, ag_sem_s, ag_sem_r, agz_sem_s, agz_sem_r):
    rows, width = x_ref.shape
    shard = w_ref.shape[0]
    state = w_ref.shape[1] // 2
    inv_root = state ** (-0.5)
    dp = lax.axis_index("dp")
    ctx = lax.axis_index("ctx")
    place = lax.rem(dp, QUAD)
    spot = dp // QUAD
    mate = {"ctx": 1 - ctx}
    quads = [{"dp": spot * QUAD + rotate(place, j, QUAD)} for j in range(1, QUAD)]
    if line <= QUAD:
        lines = [{"dp": rotate(spot, j, line) * QUAD + place} for j in range(1, line)]
    else:
        lines = []
        m = 1
        while m < line:
            lines.append({"dp": dp + QUAD * m * (1 - 2 * lax.rem(spot // m, 2))})
            m *= 2

    def send(src, dst, s_sem, r_sem, who):
        copy = pltpu.make_async_remote_copy(
            src_ref=src, dst_ref=dst, send_sem=s_sem, recv_sem=r_sem, device_id=who, device_id_type=MESH)
        copy.start()
        return copy

    loads = [pltpu.make_async_copy(a, b, in_sem.at[k])
             for k, (a, b) in enumerate(((lr_hbm, lr_ref), (w_hbm, w_ref), (x_hbm, x_ref), (g_hbm, g_ref)))]
    for load in loads:
        load.start()
    barrier = pltpu.get_barrier_semaphore()
    for who in [mate] + quads + lines:
        pl.semaphore_signal(barrier, inc=1, device_id=who, device_id_type=MESH)

    own = pl.ds(pl.multiple_of(ctx * shard, shard), shard)
    far = pl.ds(pl.multiple_of((1 - ctx) * shard, shard), shard)

    loads[0].wait()
    lr = lr_ref[...]
    ti = lax.broadcasted_iota(jnp.int32, (rows, rows), 0)
    si = lax.broadcasted_iota(jnp.int32, (rows, rows), 1)
    tri = jnp.where(ti <= si, 1.0, 0.0).astype(F32)
    lr_t = jnp.concatenate([lr, jnp.zeros((rows - head_count, rows), F32)], axis=0)
    incl_t = lax.dot_general(lr_t, tri, NN, precision=lax.Precision.HIGHEST, preferred_element_type=F32)
    excl_t = incl_t - lr_t
    lr_pad = jnp.transpose(lr_t)
    incl = jnp.transpose(incl_t)
    excl = incl - lr_pad
    total = incl[rows - 1:rows, :]
    step = jnp.sqrt(one_minus_exp(2.0 * lr_pad))
    first = ctx == 0
    rate_x = jnp.exp(jnp.where(first, total - incl, excl))
    rate_g = jnp.exp(jnp.where(first, total - excl, incl)) * inv_root
    hi_ = lax.broadcasted_iota(jnp.int32, (rows, width), 0)
    ci_ = lax.broadcasted_iota(jnp.int32, (rows, width), 1)
    head_dim = width // head_count
    lo_c = hi_ * head_dim
    spread = jnp.where((ci_ >= lo_c) & (ci_ < lo_c + head_dim), 1.0, 0.0).astype(BF16)

    def widen(v):
        top = v.astype(BF16)
        low = (v - top.astype(F32)).astype(BF16)
        return mm(top, spread) + mm(low, spread)

    quarter = shard // QUAD

    def columns(c, q, k, size):
        return pl.ds(pl.multiple_of(c * shard + q * quarter + k * 128, 128), size)

    pl.semaphore_wait(barrier, 1 + len(quads) + len(lines))
    w_copy = send(w_hbm, w_other, w_sem.at[0], w_sem.at[1], mate)
    x_copies = [send(x_hbm.at[:, columns(c, rotate(place, j, QUAD), 0, quarter)], xr.at[j - 1, c],
                     x_sem_s.at[j - 1, c], x_sem_r.at[j - 1, c], quads[j - 1])
                for j in range(1, QUAD) for c in range(2)]
    step_w = widen(step)
    gx[...] = step_w
    wide_x = widen(rate_x * step)
    loads[1].wait()
    loads[2].wait()
    xf = x_ref[...].astype(F32)
    xs[...] = (xf * step_w).astype(BF16)
    xw[...] = (xf * wide_x).astype(BF16)
    loads[3].wait()
    gs[...] = (g_ref[...].astype(F32) * widen(rate_g)).astype(BF16)

    bc = mm(x_ref[:, own], w_ref[...])
    w_copy.wait()
    bc = (bc + mm(x_ref[:, far], w_other[...])).astype(BF16)
    b_in = bc[:, :state]
    c_out = bc[:, state:]

    s_copies = []
    for k, (basis, vals) in enumerate(((b_in, xw), (c_out, gs))):
        s_send[k] = mm(flip(basis), vals[...]).astype(BF16)
        copy = pltpu.make_async_remote_copy(
            src_ref=s_send.at[k], dst_ref=s_recv.at[k], send_sem=s_sem_s.at[k], recv_sem=s_sem_r.at[k],
            device_id=mate, device_id_type=MESH)
        copy.start()
        s_copies.append(copy)

    twice = jnp.where(ti == si, 2.0, 1.0).astype(F32)
    dots = mm(b_in, c_out, NT) * (twice * inv_root)
    upper = si >= ti
    lane = lax.broadcasted_iota(jnp.int32, (rows, 2 * head_dim), 1)
    wb = jnp.zeros((rows, rows), F32)
    for pair in range(head_count // 2):
        cols = slice(pair * 2 * head_dim, (pair + 1) * 2 * head_dim)
        gp = g_ref[:, cols]
        zero = jnp.zeros_like(gp)
        gm = jnp.concatenate([jnp.where(lane < head_dim, gp, zero), jnp.where(lane < head_dim, zero, gp)], axis=0)
        cross = mm(xs[:, cols], gm, NT)
        parts = []
        for j in range(2):
            h = 2 * pair + j
            gap = jnp.where(upper, incl_t[h:h + 1, :] - incl[:, h:h + 1], excl[:, h:h + 1] - excl_t[h:h + 1, :])
            mix = jnp.exp(gap)
            wb = wb + mix * cross[:, j * rows:(j + 1) * rows]
            parts.append((mix * dots).astype(BF16))
        gx[:, cols] = gx[:, cols] * mm(jnp.concatenate(parts, axis=1), gm)
    wb = (wb * (twice * inv_root)).astype(BF16)
    grad_b = mm(wb, c_out)
    grad_c = mm(flip(wb), b_in)
    s_copies[0].wait()
    grad_c = grad_c + mm(gs[...], s_recv[0], NT)
    s_copies[1].wait()
    grad_b = grad_b + mm(xw[...], s_recv[1], NT)
    grad_bc = jnp.concatenate([grad_b, grad_c], axis=1).astype(BF16)
    bc_all[0] = grad_bc
    b_copies = [send(bc_all.at[0], bc_all.at[j], b_sem_s.at[j - 1], b_sem_r.at[j - 1], quads[j - 1])
                for j in range(1, QUAD)]

    gx[...] = mm(b_in, s_recv[1]) * wide_x + gx[...]
    gf_ref[:, own] = (gx[:, own] + mm(grad_bc, w_ref[...], NT)).astype(BF16)
    gf_ref[:, far] = (gx[:, far] + mm(grad_bc, w_other[...], NT)).astype(BF16)

    def turn(j, c):
        for k in range(quarter // 128):
            tile = x_ref[:, columns(c, place, k, 128)] if j == 0 else xr[j - 1, c, :, k * 128:(k + 1) * 128]
            xt[c, k * 128:(k + 1) * 128, j * rows:(j + 1) * rows] = flip(tile)

    for c in range(2):
        turn(0, c)
    for copy in x_copies:
        copy.wait()
    for j in range(1, QUAD):
        for c in range(2):
            turn(j, c)
    for copy in b_copies:
        copy.wait()
    right = jnp.concatenate([bc_all[j] for j in range(QUAD)], axis=0)

    def partial(c):
        return mm(xt[c], right)

    half_send[...] = partial(1 - ctx).astype(BF16)
    h_copy = send(half_send, half_recv, h_sem.at[0], h_sem.at[1], mate)
    mine = partial(ctx)
    h_copy.wait()
    mine = mine + half_recv[...].astype(F32)
    scale = total_rows ** (-0.5)
    if line <= QUAD:
        piece = quarter // line
        acc[...] = mine.reshape(line, piece, 2 * state)
        parts = 2 if piece % 32 == 0 else 1
        h = piece // parts

        def cut(p):
            return pl.ds(p * h, h)

        z_copies = []
        for p in range(parts):
            for j in range(1, line):
                z_send[j - 1, p * h:(p + 1) * h] = acc[rotate(spot, j, line), p * h:(p + 1) * h].astype(BF16)
                z_copies.append(send(z_send.at[j - 1, cut(p)], z_recv.at[j - 1, cut(p)],
                                     z_sem_s.at[j - 1, p], z_sem_r.at[j - 1, p], lines[j - 1]))
        agz, ag = [], []

        def spread_out(k, p, at):
            got = gw_ref.at[place, at, cut(p)]
            for j in range(QUAD - 1):
                ag.append(send(got, got, ag_sem_s.at[k, j, p], ag_sem_r.at[k, j, p], quads[j]))

        for p in range(parts):
            whole = acc[spot, p * h:(p + 1) * h]
            for j in range(line - 1):
                z_copies[p * (line - 1) + j].wait()
                whole = whole + z_recv[j, p * h:(p + 1) * h].astype(F32)
            gw_ref[place, spot, p * h:(p + 1) * h] = (whole * scale).astype(BF16)
            own_piece = gw_ref.at[place, spot, cut(p)]
            for j in range(1, line):
                agz.append(send(own_piece, own_piece, agz_sem_s.at[j - 1, p], agz_sem_r.at[j - 1, p], lines[j - 1]))
            spread_out(0, p, spot)
        for p in range(parts):
            for k in range(1, line):
                agz[p * (line - 1) + k - 1].wait_recv()
                spread_out(k, p, rotate(spot, line - k, line))
        for copy in agz:
            copy.wait_send()
        for copy in ag:
            copy.wait()
    else:
        for j in range(len(lines)):
            z_send[j] = mine.astype(BF16)
            copy = send(z_send.at[j], z_recv.at[j], z_sem_s.at[j, 0], z_sem_r.at[j, 0], lines[j])
            copy.wait()
            mine = z_send[j].astype(F32) + z_recv[j].astype(F32)
        gw_ref[place, 0] = (mine * scale).astype(BF16)
        got = gw_ref.at[place, 0]
        ag = [send(got, got, ag_sem_s.at[0, j, 0], ag_sem_r.at[0, j, 0], quads[j]) for j in range(QUAD - 1)]
        for copy in ag:
            copy.wait()


def per_device(dp_count, ctx_count, features, log_decays, cotangent, bc_weight):
    x, lr, g = features[0], jnp.swapaxes(log_decays[0], 0, 1), cotangent[0]
    rows, width = x.shape
    shard, cols = bc_weight.shape
    total_rows = features.shape[0] * dp_count * rows * ctx_count
    head_count = lr.shape[0]
    half = cols // 2
    line = dp_count // QUAD
    direct = line <= QUAD
    pieces = line if direct else 1
    hops = max(line - 1, 1) if direct else line.bit_length() - 1
    quarter = shard // QUAD
    piece = quarter // pieces
    dma = pltpu.SemaphoreType.DMA
    vm = pl.BlockSpec(memory_space=pltpu.VMEM)
    gf, gw = pl.pallas_call(
        functools.partial(body, line, total_rows, head_count),
        out_shape=(pltpu.VMEM((rows, width), BF16), pltpu.VMEM((QUAD, pieces, piece, cols), BF16)),
        in_specs=[pl.BlockSpec(memory_space=pltpu.HBM)] * 4,
        out_specs=(vm, vm),
        scratch_shapes=[
            pltpu.VMEM((rows, width), BF16),
            pltpu.VMEM((head_count, rows), F32),
            pltpu.VMEM((rows, width), BF16),
            pltpu.VMEM((shard, cols), BF16),
            pltpu.VMEM((shard, cols), BF16),
            pltpu.VMEM((2, quarter, QUAD * rows), BF16),
            pltpu.VMEM((QUAD - 1, 2, rows, quarter), BF16),
            pltpu.VMEM((rows, width), BF16),
            pltpu.VMEM((rows, width), BF16),
            pltpu.VMEM((rows, width), BF16),
            pltpu.VMEM((2, half, width), BF16),
            pltpu.VMEM((2, half, width), BF16),
            pltpu.VMEM((rows, width), F32),
            pltpu.VMEM((QUAD, rows, cols), BF16),
            pltpu.VMEM((pieces, piece, cols), F32),
            pltpu.VMEM((quarter, cols), BF16),
            pltpu.VMEM((quarter, cols), BF16),
            pltpu.VMEM((hops, piece, cols), BF16),
            pltpu.VMEM((hops, piece, cols), BF16),
            dma((4,)), dma((2,)), dma((2,)), dma((2,)),
            dma((QUAD - 1, 2)), dma((QUAD - 1, 2)), dma((QUAD - 1,)), dma((QUAD - 1,)), dma((2,)),
            dma((hops, 2)), dma((hops, 2)),
            dma((pieces, QUAD - 1, 2)), dma((pieces, QUAD - 1, 2)), dma((hops, 2)), dma((hops, 2)),
        ],
        compiler_params=pltpu.CompilerParams(
            collective_id=0, has_side_effects=True, vmem_limit_bytes=64256 * 1024),
    )(x, lr, g, bc_weight)
    gw = gw.reshape(shard, cols)
    return gf[None], gw


def solution(mesh):
    placed = (P("dp", "ctx", None), P("dp", "ctx", None), P("dp", "ctx", None), P("ctx", None))
    return jax.shard_map(
        functools.partial(per_device, mesh.shape["dp"], mesh.shape["ctx"]),
        mesh=mesh,
        in_specs=placed,
        out_specs=(P("dp", "ctx", None), P("ctx", None)),
        check_vma=False,
    )
```

```python
import functools

import jax
import jax.numpy as jnp
from jax import lax
from jax.experimental import pallas as pl
from jax.experimental.pallas import tpu as pltpu
from jax.sharding import PartitionSpec as P

MESH = pl.DeviceIdType.MESH
F32 = jnp.float32
BF16 = jnp.bfloat16
NN = (((1,), (0,)), ((), ()))
NT = (((1,), (1,)), ((), ()))
QUAD = 4


def mm(a, b, dims=NN):
    return lax.dot_general(a, b, dims, preferred_element_type=F32)


def flip(a):
    return jnp.transpose(a.astype(F32)).astype(a.dtype)


def one_minus_exp(y):
    z = y * 0.125
    f = z * (1.0 + z * (1 / 2) * (1.0 + z * (1 / 3) * (1.0 + z * (1 / 4) * (1.0 + z * (1 / 5) * (1.0 + z * (1 / 6) * (1.0 + z * (1 / 7)))))))
    for _ in range(3):
        f = f * (f + 2.0)
    return -f


def partner(place, j):
    out, bit = place, 1
    while bit <= j:
        if j & bit:
            out = out + bit - 2 * bit * lax.rem(place // bit, 2)
        bit *= 2
    return out


def body(line, total_rows, head_count, x_hbm, lr_hbm, g_hbm, w_hbm, gf_ref, gw_ref,
         x_ref, lr_ref, g_ref, w_ref, w_other, xt, xr, xs, xw, gs, s_send, s_recv, gx, bc_all,
         pm, acc, half_send, half_recv, z_send, z_recv,
         in_sem, w_sem, s_sem_s, s_sem_r, x_sem_s, x_sem_r, b_sem_s, b_sem_r, h_sem,
         z_sem_s, z_sem_r, ag_sem_s, ag_sem_r, agz_sem_s, agz_sem_r):
    rows, width = x_ref.shape
    shard = w_ref.shape[0]
    state = w_ref.shape[1] // 2
    inv_root = state ** (-0.5)
    dp = lax.axis_index("dp")
    ctx = lax.axis_index("ctx")
    place = lax.rem(dp, QUAD)
    spot = dp // QUAD
    mate = {"ctx": 1 - ctx}
    far_first = (3, 2, 1)
    quads = [{"dp": spot * QUAD + partner(place, j)} for j in range(1, QUAD)]
    if line <= QUAD:
        lines = [{"dp": partner(spot, j) * QUAD + place} for j in range(1, line)]
    else:
        lines = []
        m = 1
        while m < line:
            lines.append({"dp": dp + QUAD * m * (1 - 2 * lax.rem(spot // m, 2))})
            m *= 2

    def send(src, dst, s_sem, r_sem, who):
        copy = pltpu.make_async_remote_copy(
            src_ref=src, dst_ref=dst, send_sem=s_sem, recv_sem=r_sem, device_id=who, device_id_type=MESH)
        copy.start()
        return copy

    loads = [pltpu.make_async_copy(a, b, in_sem.at[k])
             for k, (a, b) in enumerate(((lr_hbm, lr_ref), (w_hbm, w_ref), (x_hbm, x_ref), (g_hbm, g_ref)))]
    for load in loads:
        load.start()
    barrier = pltpu.get_barrier_semaphore()
    for who in [mate] + quads + lines:
        pl.semaphore_signal(barrier, inc=1, device_id=who, device_id_type=MESH)

    own = pl.ds(pl.multiple_of(ctx * shard, shard), shard)
    far = pl.ds(pl.multiple_of((1 - ctx) * shard, shard), shard)

    quarter = shard // QUAD

    def columns(c, q, k, size):
        return pl.ds(pl.multiple_of(c * shard + q * quarter + k * 128, 128), size)

    pl.semaphore_wait(barrier, 1 + len(quads) + len(lines))
    w_copy = send(w_hbm, w_other, w_sem.at[0], w_sem.at[1], mate)
    x_copies = [send(x_hbm.at[:, columns(c, partner(place, j), 0, quarter)], xr.at[j - 1, c],
                     x_sem_s.at[j - 1, c], x_sem_r.at[j - 1, c], quads[j - 1])
                for j in far_first for c in range(2)]

    loads[0].wait()
    lr = lr_ref[...]
    ti = lax.broadcasted_iota(jnp.int32, (rows, rows), 0)
    si = lax.broadcasted_iota(jnp.int32, (rows, rows), 1)
    tri = jnp.where(ti <= si, 1.0, 0.0).astype(F32)
    lr_t = jnp.concatenate([lr, jnp.zeros((rows - head_count, rows), F32)], axis=0)
    incl_t = lax.dot_general(lr_t, tri, NN, precision=lax.Precision.HIGHEST, preferred_element_type=F32)
    excl_t = incl_t - lr_t
    lr_pad = jnp.transpose(lr_t)
    incl = jnp.transpose(incl_t)
    excl = incl - lr_pad
    total = incl[rows - 1:rows, :]
    step = jnp.sqrt(one_minus_exp(2.0 * lr_pad))
    first = ctx == 0
    rate_x = jnp.exp(jnp.where(first, total - incl, excl))
    rate_g = jnp.exp(jnp.where(first, total - excl, incl)) * inv_root
    hi_ = lax.broadcasted_iota(jnp.int32, (rows, width), 0)
    ci_ = lax.broadcasted_iota(jnp.int32, (rows, width), 1)
    head_dim = width // head_count
    lo_c = hi_ * head_dim
    spread = jnp.where((ci_ >= lo_c) & (ci_ < lo_c + head_dim), 1.0, 0.0).astype(BF16)

    def widen(v):
        top = v.astype(BF16)
        low = (v - top.astype(F32)).astype(BF16)
        return mm(top, spread) + mm(low, spread)

    step_w = widen(step)
    gx[...] = step_w
    wide_x = widen(rate_x * step)
    loads[1].wait()
    loads[2].wait()
    xf = x_ref[...].astype(F32)
    xs[...] = (xf * step_w).astype(BF16)
    xw[...] = (xf * wide_x).astype(BF16)
    loads[3].wait()
    gs[...] = (g_ref[...].astype(F32) * widen(rate_g)).astype(BF16)

    bc = mm(x_ref[:, own], w_ref[...])
    w_copy.wait()
    bc = (bc + mm(x_ref[:, far], w_other[...])).astype(BF16)
    b_in = bc[:, :state]
    c_out = bc[:, state:]

    s_copies = []
    for k, (basis, vals) in enumerate(((b_in, xw), (c_out, gs))):
        s_send[k] = mm(flip(basis), vals[...]).astype(BF16)
        copy = pltpu.make_async_remote_copy(
            src_ref=s_send.at[k], dst_ref=s_recv.at[k], send_sem=s_sem_s.at[k], recv_sem=s_sem_r.at[k],
            device_id=mate, device_id_type=MESH)
        copy.start()
        s_copies.append(copy)

    twice = jnp.where(ti == si, 2.0, 1.0).astype(F32)
    dots = mm(b_in, c_out, NT) * (twice * inv_root)
    upper = si >= ti
    lane = lax.broadcasted_iota(jnp.int32, (rows, 2 * head_dim), 1)

    def apart(cols):
        gp = g_ref[:, cols]
        zero = jnp.zeros_like(gp)
        return jnp.concatenate([jnp.where(lane < head_dim, gp, zero), jnp.where(lane < head_dim, zero, gp)], axis=0)

    wb = jnp.zeros((rows, rows), F32)
    for pair in range(head_count // 2):
        cols = slice(pair * 2 * head_dim, (pair + 1) * 2 * head_dim)
        cross = mm(xs[:, cols], apart(cols), NT)
        for j in range(2):
            h = 2 * pair + j
            gap = jnp.where(upper, incl_t[h:h + 1, :] - incl[:, h:h + 1], excl[:, h:h + 1] - excl_t[h:h + 1, :])
            mix = jnp.exp(gap)
            wb = wb + mix * cross[:, j * rows:(j + 1) * rows]
            pm[pair, :, j * rows:(j + 1) * rows] = (mix * dots).astype(BF16)
    wb = (wb * (twice * inv_root)).astype(BF16)
    grad_b = mm(wb, c_out)
    grad_c = mm(flip(wb), b_in)
    s_copies[0].wait()
    grad_c = grad_c + mm(gs[...], s_recv[0], NT)
    s_copies[1].wait()
    grad_b = grad_b + mm(xw[...], s_recv[1], NT)
    grad_bc = jnp.concatenate([grad_b, grad_c], axis=1).astype(BF16)
    bc_all[0] = grad_bc
    b_copies = [send(bc_all.at[0], bc_all.at[j], b_sem_s.at[j - 1], b_sem_r.at[j - 1], quads[j - 1])
                for j in far_first]

    def finish_features():
        for pair in range(head_count // 2):
            cols = slice(pair * 2 * head_dim, (pair + 1) * 2 * head_dim)
            gx[:, cols] = gx[:, cols] * mm(pm[pair], apart(cols))
        gx[...] = mm(b_in, s_recv[1]) * wide_x + gx[...]
        gf_ref[:, own] = (gx[:, own] + mm(grad_bc, w_ref[...], NT)).astype(BF16)
        gf_ref[:, far] = (gx[:, far] + mm(grad_bc, w_other[...], NT)).astype(BF16)

    finish_features()

    def turn(j, c):
        for k in range(quarter // 128):
            tile = x_ref[:, columns(c, place, k, 128)] if j == 0 else xr[j - 1, c, :, k * 128:(k + 1) * 128]
            xt[c, k * 128:(k + 1) * 128, j * rows:(j + 1) * rows] = flip(tile)

    for c in range(2):
        turn(0, c)
    for copy in x_copies:
        copy.wait()
    for j in range(1, QUAD):
        for c in range(2):
            turn(j, c)
    for copy in b_copies:
        copy.wait()
    right = jnp.concatenate([bc_all[j] for j in range(QUAD)], axis=0)

    def partial(c):
        return mm(xt[c], right)

    half_send[...] = partial(1 - ctx).astype(BF16)
    h_copy = send(half_send, half_recv, h_sem.at[0], h_sem.at[1], mate)
    mine = partial(ctx)
    h_copy.wait()
    mine = mine + half_recv[...].astype(F32)
    scale = total_rows ** (-0.5)
    if line <= QUAD:
        piece = quarter // line
        acc[...] = mine.reshape(line, piece, 2 * state)
        parts = 2 if piece % 32 == 0 else 1
        h = piece // parts

        def cut(p):
            return pl.ds(p * h, h)

        order = range(1, line)
        z_copies = {}
        for p in range(parts):
            for j in reversed(order):
                z_send[j - 1, p * h:(p + 1) * h] = acc[partner(spot, j), p * h:(p + 1) * h].astype(BF16)
                z_copies[j, p] = send(z_send.at[j - 1, cut(p)], z_recv.at[j - 1, cut(p)],
                                      z_sem_s.at[j - 1, p], z_sem_r.at[j - 1, p], lines[j - 1])
        agz, ag = {}, []

        def spread_out(k, p, at):
            got = gw_ref.at[place, at, cut(p)]
            for j in far_first:
                ag.append(send(got, got, ag_sem_s.at[k, j - 1, p], ag_sem_r.at[k, j - 1, p], quads[j - 1]))

        for p in range(parts):
            whole = acc[spot, p * h:(p + 1) * h]
            for j in order:
                z_copies[j, p].wait()
                whole = whole + z_recv[j - 1, p * h:(p + 1) * h].astype(F32)
            gw_ref[place, spot, p * h:(p + 1) * h] = (whole * scale).astype(BF16)
            own_piece = gw_ref.at[place, spot, cut(p)]
            for j in reversed(order):
                agz[j, p] = send(own_piece, own_piece, agz_sem_s.at[j - 1, p], agz_sem_r.at[j - 1, p], lines[j - 1])
            spread_out(0, p, spot)
        for p in range(parts):
            for j in order:
                agz[j, p].wait_recv()
                spread_out(j, p, partner(spot, j))
        for copy in agz.values():
            copy.wait_send()
        for copy in ag:
            copy.wait()
    else:
        for j in range(len(lines)):
            z_send[j] = mine.astype(BF16)
            copy = send(z_send.at[j], z_recv.at[j], z_sem_s.at[j, 0], z_sem_r.at[j, 0], lines[j])
            copy.wait()
            mine = z_send[j].astype(F32) + z_recv[j].astype(F32)
        gw_ref[place, 0] = (mine * scale).astype(BF16)
        got = gw_ref.at[place, 0]
        ag = [send(got, got, ag_sem_s.at[0, j, 0], ag_sem_r.at[0, j, 0], quads[j]) for j in range(QUAD - 1)]
        for copy in ag:
            copy.wait()


def deliver(gf_ref, gw_ref, gf_hbm, gw_hbm, sem):
    copies = [pltpu.make_async_copy(a, b, sem.at[k]) for k, (a, b) in enumerate(((gf_ref, gf_hbm), (gw_ref, gw_hbm)))]
    for copy in copies:
        copy.start()
    for copy in copies:
        copy.wait()


def per_device(dp_count, ctx_count, features, log_decays, cotangent, bc_weight):
    x, lr, g = features[0], jnp.swapaxes(log_decays[0], 0, 1), cotangent[0]
    rows, width = x.shape
    shard, cols = bc_weight.shape
    total_rows = features.shape[0] * dp_count * rows * ctx_count
    head_count = lr.shape[0]
    half = cols // 2
    line = dp_count // QUAD
    direct = line <= QUAD
    pieces = line if direct else 1
    hops = max(line - 1, 1) if direct else line.bit_length() - 1
    quarter = shard // QUAD
    piece = quarter // pieces
    dma = pltpu.SemaphoreType.DMA
    vm = pl.BlockSpec(memory_space=pltpu.VMEM)
    gf, gw = pl.pallas_call(
        functools.partial(body, line, total_rows, head_count),
        out_shape=(pltpu.VMEM((rows, width), BF16), pltpu.VMEM((QUAD, pieces, piece, cols), BF16)),
        in_specs=[pl.BlockSpec(memory_space=pltpu.HBM)] * 4,
        out_specs=(vm, vm),
        scratch_shapes=[
            pltpu.VMEM((rows, width), BF16),
            pltpu.VMEM((head_count, rows), F32),
            pltpu.VMEM((rows, width), BF16),
            pltpu.VMEM((shard, cols), BF16),
            pltpu.VMEM((shard, cols), BF16),
            pltpu.VMEM((2, quarter, QUAD * rows), BF16),
            pltpu.VMEM((QUAD - 1, 2, rows, quarter), BF16),
            pltpu.VMEM((rows, width), BF16),
            pltpu.VMEM((rows, width), BF16),
            pltpu.VMEM((rows, width), BF16),
            pltpu.VMEM((2, half, width), BF16),
            pltpu.VMEM((2, half, width), BF16),
            pltpu.VMEM((rows, width), F32),
            pltpu.VMEM((QUAD, rows, cols), BF16),
            pltpu.VMEM((head_count // 2, rows, 2 * rows), BF16),
            pltpu.VMEM((pieces, piece, cols), F32),
            pltpu.VMEM((quarter, cols), BF16),
            pltpu.VMEM((quarter, cols), BF16),
            pltpu.VMEM((hops, piece, cols), BF16),
            pltpu.VMEM((hops, piece, cols), BF16),
            dma((4,)), dma((2,)), dma((2,)), dma((2,)),
            dma((QUAD - 1, 2)), dma((QUAD - 1, 2)), dma((QUAD - 1,)), dma((QUAD - 1,)), dma((2,)),
            dma((hops, 2)), dma((hops, 2)),
            dma((pieces, QUAD - 1, 2)), dma((pieces, QUAD - 1, 2)), dma((hops, 2)), dma((hops, 2)),
        ],
        compiler_params=pltpu.CompilerParams(
            collective_id=0, has_side_effects=True, vmem_limit_bytes=64256 * 1024),
    )(x, lr, g, bc_weight)
    gw = gw.reshape(shard, cols)
    hbm = pl.BlockSpec(memory_space=pltpu.HBM)
    gf, gw = pl.pallas_call(
        deliver,
        out_shape=(jax.ShapeDtypeStruct((rows, width), BF16), jax.ShapeDtypeStruct((shard, cols), BF16)),
        in_specs=[vm, vm],
        out_specs=(hbm, hbm),
        scratch_shapes=[dma((2,))],
        compiler_params=pltpu.CompilerParams(vmem_limit_bytes=2 * 2**20),
    )(gf, gw)
    return gf[None], gw


def solution(mesh):
    placed = (P("dp", "ctx", None), P("dp", "ctx", None), P("dp", "ctx", None), P("ctx", None))
    return jax.shard_map(
        functools.partial(per_device, mesh.shape["dp"], mesh.shape["ctx"]),
        mesh=mesh,
        in_specs=placed,
        out_specs=(P("dp", "ctx", None), P("ctx", None)),
        check_vma=False,
    )
```

```python
import functools

import jax
import jax.numpy as jnp
from jax import lax
from jax.experimental import pallas as pl
from jax.experimental.pallas import tpu as pltpu
from jax.sharding import PartitionSpec as P

MESH = pl.DeviceIdType.MESH
F32 = jnp.float32
BF16 = jnp.bfloat16
NN = (((1,), (0,)), ((), ()))
NT = (((1,), (1,)), ((), ()))
QUAD = 4


def mm(a, b, dims=NN):
    return lax.dot_general(a, b, dims, preferred_element_type=F32)


def flip(a):
    return jnp.transpose(a.astype(F32)).astype(a.dtype)


def one_minus_exp(y):
    z = y * 0.125
    f = z * (1.0 + z * (1 / 2) * (1.0 + z * (1 / 3) * (1.0 + z * (1 / 4) * (1.0 + z * (1 / 5) * (1.0 + z * (1 / 6) * (1.0 + z * (1 / 7)))))))
    for _ in range(3):
        f = f * (f + 2.0)
    return -f


def partner(place, j):
    out, bit = place, 1
    while bit <= j:
        if j & bit:
            out = out + bit - 2 * bit * lax.rem(place // bit, 2)
        bit *= 2
    return out


def body(line, total_rows, head_count, x_hbm, lr_hbm, g_hbm, w_hbm, gf_ref, gw_ref,
         x_ref, lr_ref, g_ref, w_ref, w_other, xr, xs, xw, gs, s_send, s_recv, gx, bc_all,
         pm, acc, z_send, z_recv, full,
         in_sem, w_sem, s_sem_s, s_sem_r, x_sem_s, x_sem_r, o_sem, b_sem_s, b_sem_r,
         z_sem_s, z_sem_r, agz_sem_s, agz_sem_r, ag_sem_s, ag_sem_r, m_sem_s, m_sem_r):
    rows, width = x_ref.shape
    shard = w_ref.shape[0]
    state = w_ref.shape[1] // 2
    inv_root = state ** (-0.5)
    dp = lax.axis_index("dp")
    ctx = lax.axis_index("ctx")
    place = lax.rem(dp, QUAD)
    spot = dp // QUAD
    blocks = acc.shape[0]
    per_shard = blocks // 2
    mate = {"ctx": 1 - ctx}
    far_first = (3, 2, 1)
    hubs = [{"dp": spot * QUAD + partner(place, j), "ctx": 1} for j in range(1, QUAD)]
    leaves = [{"dp": spot * QUAD + partner(place, j), "ctx": 0} for j in range(1, QUAD)]
    if line == blocks:
        lines = [{"dp": partner(spot, j) * QUAD + place} for j in range(1, line)]
    else:
        lines = []
        m = 1
        while m < line:
            lines.append({"dp": dp + QUAD * m * (1 - 2 * lax.rem(spot // m, 2))})
            m *= 2

    def remote(src, dst, s_sem, r_sem, who):
        return pltpu.make_async_remote_copy(
            src_ref=src, dst_ref=dst, send_sem=s_sem, recv_sem=r_sem, device_id=who, device_id_type=MESH)

    def send(src, dst, s_sem, r_sem, who):
        copy = remote(src, dst, s_sem, r_sem, who)
        copy.start()
        return copy

    loads = [pltpu.make_async_copy(a, b, in_sem.at[k])
             for k, (a, b) in enumerate(((lr_hbm, lr_ref), (w_hbm, w_ref), (x_hbm, x_ref), (g_hbm, g_ref)))]
    for load in loads:
        load.start()
    barrier = pltpu.get_barrier_semaphore()
    for who in [mate] + hubs:
        pl.semaphore_signal(barrier, inc=1, device_id=who, device_id_type=MESH)

    @pl.when(ctx == 1)
    def _():
        for who in leaves + lines:
            pl.semaphore_signal(barrier, inc=1, device_id=who, device_id_type=MESH)

    own = pl.ds(pl.multiple_of(ctx * shard, shard), shard)
    far = pl.ds(pl.multiple_of((1 - ctx) * shard, shard), shard)

    quarter = shard // QUAD

    def columns(c, q):
        return pl.ds(pl.multiple_of(c * shard + q * quarter, quarter), quarter)

    def strip(c):
        return slice(c * quarter, (c + 1) * quarter)

    def band(k):
        return pl.ds(pl.multiple_of(k * rows, rows), rows)

    pl.semaphore_wait(barrier, QUAD + ctx * (QUAD - 1 + len(lines)))
    w_copy = send(w_hbm, w_other, w_sem.at[0], w_sem.at[1], mate)

    def x_copy(j, c, source, who):
        return remote(x_hbm.at[:, columns(c, partner(place, j))], xr.at[j, band(source), strip(c)],
                      x_sem_s.at[j, c], x_sem_r.at[j, source, c], who)

    x_copies = [x_copy(j, c, ctx, hubs[j - 1]) for j in far_first for c in range(2)]
    for copy in x_copies:
        copy.start()
    own_copies = [pltpu.make_async_copy(x_hbm.at[:, columns(c, place)], xr.at[0, band(ctx), strip(c)], o_sem.at[c])
                  for c in range(2)]
    mate_copies = [x_copy(0, c, 0, mate) for c in range(2)]

    @pl.when(ctx == 1)
    def _():
        for copy in own_copies:
            copy.start()

    @pl.when(ctx == 0)
    def _():
        for copy in mate_copies:
            copy.start()

    loads[0].wait()
    lr = lr_ref[...]
    ti = lax.broadcasted_iota(jnp.int32, (rows, rows), 0)
    si = lax.broadcasted_iota(jnp.int32, (rows, rows), 1)
    tri = jnp.where(ti <= si, 1.0, 0.0).astype(F32)
    lr_t = jnp.concatenate([lr, jnp.zeros((rows - head_count, rows), F32)], axis=0)
    incl_t = lax.dot_general(lr_t, tri, NN, precision=lax.Precision.HIGHEST, preferred_element_type=F32)
    excl_t = incl_t - lr_t
    lr_pad = jnp.transpose(lr_t)
    incl = jnp.transpose(incl_t)
    excl = incl - lr_pad
    total = incl[rows - 1:rows, :]
    step = jnp.sqrt(one_minus_exp(2.0 * lr_pad))
    first = ctx == 0
    rate_x = jnp.exp(jnp.where(first, total - incl, excl))
    rate_g = jnp.exp(jnp.where(first, total - excl, incl)) * inv_root
    hi_ = lax.broadcasted_iota(jnp.int32, (rows, width), 0)
    ci_ = lax.broadcasted_iota(jnp.int32, (rows, width), 1)
    head_dim = width // head_count
    lo_c = hi_ * head_dim
    spread = jnp.where((ci_ >= lo_c) & (ci_ < lo_c + head_dim), 1.0, 0.0).astype(BF16)

    def widen(v):
        top = v.astype(BF16)
        low = (v - top.astype(F32)).astype(BF16)
        return mm(top, spread) + mm(low, spread)

    step_w = widen(step)
    gx[...] = step_w
    wide_x = widen(rate_x * step)
    loads[1].wait()
    loads[2].wait()
    xf = x_ref[...].astype(F32)
    xs[...] = (xf * step_w).astype(BF16)
    xw[...] = (xf * wide_x).astype(BF16)
    loads[3].wait()
    gs[...] = (g_ref[...].astype(F32) * widen(rate_g)).astype(BF16)

    bc = mm(x_ref[:, own], w_ref[...])
    w_copy.wait()
    bc = (bc + mm(x_ref[:, far], w_other[...])).astype(BF16)
    b_in = bc[:, :state]
    c_out = bc[:, state:]

    s_copies = []
    b_t, c_t = flip(b_in), flip(c_out)
    for k, (basis, vals) in enumerate(((b_t, xw), (c_t, gs))):
        s_send[k] = mm(basis, vals[...]).astype(BF16)
        copy = pltpu.make_async_remote_copy(
            src_ref=s_send.at[k], dst_ref=s_recv.at[k], send_sem=s_sem_s.at[k], recv_sem=s_sem_r.at[k],
            device_id=mate, device_id_type=MESH)
        copy.start()
        s_copies.append(copy)

    twice = jnp.where(ti == si, 2.0, 1.0).astype(F32)
    dots = mm(b_in, c_out, NT) * (twice * inv_root)
    upper = si >= ti
    lane = lax.broadcasted_iota(jnp.int32, (rows, 2 * head_dim), 1)

    def apart(cols):
        gp = g_ref[:, cols]
        zero = jnp.zeros_like(gp)
        return jnp.concatenate([jnp.where(lane < head_dim, gp, zero), jnp.where(lane < head_dim, zero, gp)], axis=0)

    wb = jnp.zeros((rows, rows), F32)
    for pair in range(head_count // 2):
        cols = slice(pair * 2 * head_dim, (pair + 1) * 2 * head_dim)
        cross = mm(xs[:, cols], apart(cols), NT)
        for j in range(2):
            h = 2 * pair + j
            gap = jnp.where(upper, incl_t[h:h + 1, :] - incl[:, h:h + 1], excl[:, h:h + 1] - excl_t[h:h + 1, :])
            mix = jnp.exp(gap)
            wb = wb + mix * cross[:, j * rows:(j + 1) * rows]
            pm[pair, :, j * rows:(j + 1) * rows] = (mix * dots).astype(BF16)
    wb = (wb * (twice * inv_root)).astype(BF16)
    grad_b = mm(c_t, wb, NT)
    grad_c = mm(b_t, wb)
    s_copies[0].wait()
    grad_c = grad_c + mm(s_recv[0], gs[...], NT)
    s_copies[1].wait()
    grad_b = grad_b + mm(s_recv[1], xw[...], NT)
    grad_bc = jnp.concatenate([grad_b, grad_c], axis=0).astype(BF16)
    bc_all[0, :, band(ctx)] = grad_bc

    def b_copy(j, source, who):
        return remote(bc_all.at[0, :, band(source)], bc_all.at[j, :, band(source)],
                      b_sem_s.at[j], b_sem_r.at[j, source], who)

    b_copies = [b_copy(j, ctx, hubs[j - 1]) for j in far_first]
    for copy in b_copies:
        copy.start()
    mate_copies.append(b_copy(0, 0, mate))

    @pl.when(ctx == 0)
    def _():
        mate_copies[2].start()

    def finish_features():
        for pair in range(head_count // 2):
            cols = slice(pair * 2 * head_dim, (pair + 1) * 2 * head_dim)
            gx[:, cols] = gx[:, cols] * mm(pm[pair], apart(cols))
        gx[...] = mm(b_in, s_recv[1]) * wide_x + gx[...]
        left = flip(grad_bc)
        gf_ref[:, own] = (gx[:, own] + mm(left, w_ref[...], NT)).astype(BF16)
        gf_ref[:, far] = (gx[:, far] + mm(left, w_other[...], NT)).astype(BF16)

    finish_features()

    scale = total_rows ** (-0.5)
    parts = 2
    h = 2 * state // parts
    parts_of = [slice(p * h, (p + 1) * h) for p in range(parts)]
    size = acc.shape[2]

    def gather_copy(j, t, p, k):
        return remote(full.at[j, :, parts_of[p]], gw_ref.at[place, lax.rem(t, per_shard), :, parts_of[p]],
                      ag_sem_s.at[j, k - 1, p], ag_sem_r.at[k - 1, lax.rem(t, per_shard), p],
                      {"dp": spot * QUAD + partner(place, k), "ctx": t // per_shard})

    def mate_copy(j, t, p):
        return remote(full.at[j, :, parts_of[p]], gw_ref.at[place, lax.rem(t, per_shard), :, parts_of[p]],
                      m_sem_s.at[j, p], m_sem_r.at[lax.rem(t, per_shard), p], {"ctx": 0})

    def spread_out(j, t, p):
        for k in far_first:
            gather_copy(j, t, p, k).start()

        @pl.when(t < per_shard)
        def _():
            mate_copy(j, t, p).start()

        @pl.when(t >= per_shard)
        def _():
            gw_ref[place, lax.rem(t, per_shard), :, parts_of[p]] = full[j, :, parts_of[p]]

    def turned(v):
        return jnp.transpose(v * scale).astype(BF16)

    @pl.when(ctx == 1)
    def _():
        for copy in own_copies:
            copy.wait()
        for c in range(2):
            mate_copies[c].wait_recv()
        mate_copies[2].wait_recv()
        for j in far_first:
            for source in range(2):
                for c in range(2):
                    x_copy(j, c, source, hubs[j - 1]).wait_recv()
        total_t = mm(bc_all[0], xr[0])
        for j in far_first:
            for source in range(2):
                b_copy(j, source, hubs[j - 1]).wait_recv()
        for j in far_first:
            total_t = total_t + mm(bc_all[j], xr[j])
        for t in range(blocks):
            acc[t] = total_t[:, t * size:(t + 1) * size]

        if line == blocks:
            order = range(1, line)
            owner = [partner(spot, j) for j in range(line)]

            def z_copy(j, p):
                return remote(z_send.at[j - 1, 0, parts_of[p]], z_recv.at[j - 1, 0, parts_of[p]],
                              z_sem_s.at[j - 1, p], z_sem_r.at[j - 1, p], lines[j - 1])

            def along(j, p):
                return remote(full.at[0, :, parts_of[p]], full.at[j, :, parts_of[p]],
                              agz_sem_s.at[j - 1, p], agz_sem_r.at[j - 1, p], lines[j - 1])

            for p in range(parts):
                for j in reversed(order):
                    z_send[j - 1, 0, parts_of[p]] = acc[owner[j], parts_of[p]].astype(BF16)
                    z_copy(j, p).start()
            for p in range(parts):
                whole = acc[spot, parts_of[p]]
                for j in order:
                    z_copy(j, p).wait_recv()
                    whole = whole + z_recv[j - 1, 0, parts_of[p]].astype(F32)
                full[0, :, parts_of[p]] = turned(whole)
                for j in reversed(order):
                    along(j, p).start()
                spread_out(0, spot, p)
            for p in range(parts):
                for j in order:
                    along(j, p).wait_recv()
                    spread_out(j, owner[j], p)
            for p in range(parts):
                for j in order:
                    z_copy(j, p).wait_send()
                    along(j, p).wait_send()
        else:
            owner = [jnp.int32(t) for t in range(blocks)]
            for k in range(len(lines)):
                z_send[k] = acc[...].astype(BF16)
                copy = send(z_send.at[k], z_recv.at[k], z_sem_s.at[k, 0], z_sem_r.at[k, 0], lines[k])
                copy.wait()
                acc[...] = z_send[k].astype(F32) + z_recv[k].astype(F32)
            for t in range(blocks):
                for p in range(parts):
                    full[t, :, parts_of[p]] = turned(acc[t, parts_of[p]])
                    spread_out(t, owner[t], p)
        for j in range(blocks):
            for p in range(parts):
                for k in far_first:
                    gather_copy(j, owner[j], p, k).wait_send()

                @pl.when(owner[j] < per_shard)
                def _():
                    mate_copy(j, owner[j], p).wait_send()

    for k in far_first:
        for i in range(per_shard):
            for p in range(parts):
                gather_copy(0, i, p, k).wait_recv()
    for copy in x_copies + b_copies:
        copy.wait_send()

    @pl.when(ctx == 0)
    def _():
        for copy in mate_copies:
            copy.wait_send()
        for i in range(per_shard):
            for p in range(parts):
                mate_copy(0, i, p).wait_recv()


def deliver(gf_ref, gw_ref, gf_hbm, gw_hbm, sem):
    copies = [pltpu.make_async_copy(a, b, sem.at[k]) for k, (a, b) in enumerate(((gf_ref, gf_hbm), (gw_ref, gw_hbm)))]
    for copy in copies:
        copy.start()
    for copy in copies:
        copy.wait()


def per_device(dp_count, ctx_count, features, log_decays, cotangent, bc_weight):
    x, lr, g = features[0], jnp.swapaxes(log_decays[0], 0, 1), cotangent[0]
    rows, width = x.shape
    shard, cols = bc_weight.shape
    total_rows = features.shape[0] * dp_count * rows * ctx_count
    head_count = lr.shape[0]
    half = cols // 2
    line = dp_count // QUAD
    quarter = shard // QUAD
    size = 128
    blocks = 2 * quarter // size
    direct = line == blocks
    hops = max(line - 1 if direct else line.bit_length() - 1, 1)
    deep = 1 if direct else blocks
    dma = pltpu.SemaphoreType.DMA
    vm = pl.BlockSpec(memory_space=pltpu.VMEM)
    gf, gw = pl.pallas_call(
        functools.partial(body, line, total_rows, head_count),
        out_shape=(pltpu.VMEM((rows, width), BF16), pltpu.VMEM((QUAD, blocks // 2, size, cols), BF16)),
        in_specs=[pl.BlockSpec(memory_space=pltpu.HBM)] * 4,
        out_specs=(vm, vm),
        scratch_shapes=[
            pltpu.VMEM((rows, width), BF16),
            pltpu.VMEM((head_count, rows), F32),
            pltpu.VMEM((rows, width), BF16),
            pltpu.VMEM((shard, cols), BF16),
            pltpu.VMEM((shard, cols), BF16),
            pltpu.VMEM((QUAD, 2 * rows, 2 * quarter), BF16),
            pltpu.VMEM((rows, width), BF16),
            pltpu.VMEM((rows, width), BF16),
            pltpu.VMEM((rows, width), BF16),
            pltpu.VMEM((2, half, width), BF16),
            pltpu.VMEM((2, half, width), BF16),
            pltpu.VMEM((rows, width), F32),
            pltpu.VMEM((QUAD, cols, 2 * rows), BF16),
            pltpu.VMEM((head_count // 2, rows, 2 * rows), BF16),
            pltpu.VMEM((blocks, cols, size), F32),
            pltpu.VMEM((hops, deep, cols, size), BF16),
            pltpu.VMEM((hops, deep, cols, size), BF16),
            pltpu.VMEM((blocks, size, cols), BF16),
            dma((4,)), dma((2,)), dma((2,)), dma((2,)),
            dma((QUAD, 2)), dma((QUAD, 2, 2)), dma((2,)), dma((QUAD,)), dma((QUAD, 2)),
            dma((hops, 2)), dma((hops, 2)), dma((hops, 2)), dma((hops, 2)),
            dma((blocks, QUAD - 1, 2)), dma((QUAD - 1, blocks // 2, 2)), dma((blocks, 2)), dma((blocks // 2, 2)),
        ],
        compiler_params=pltpu.CompilerParams(
            collective_id=0, has_side_effects=True, vmem_limit_bytes=64256 * 1024),
    )(x, lr, g, bc_weight)
    gw = gw.reshape(shard, cols)
    hbm = pl.BlockSpec(memory_space=pltpu.HBM)
    gf, gw = pl.pallas_call(
        deliver,
        out_shape=(jax.ShapeDtypeStruct((rows, width), BF16), jax.ShapeDtypeStruct((shard, cols), BF16)),
        in_specs=[vm, vm],
        out_specs=(hbm, hbm),
        scratch_shapes=[dma((2,))],
        compiler_params=pltpu.CompilerParams(vmem_limit_bytes=2 * 2**20),
    )(gf, gw)
    return gf[None], gw


def solution(mesh):
    placed = (P("dp", "ctx", None), P("dp", "ctx", None), P("dp", "ctx", None), P("ctx", None))
    return jax.shard_map(
        functools.partial(per_device, mesh.shape["dp"], mesh.shape["ctx"]),
        mesh=mesh,
        in_specs=placed,
        out_specs=(P("dp", "ctx", None), P("ctx", None)),
        check_vma=False,
    )
```

```python
import functools

import jax
import jax.numpy as jnp
from jax import lax
from jax.experimental import pallas as pl
from jax.experimental.pallas import tpu as pltpu
from jax.sharding import PartitionSpec as P

MESH = pl.DeviceIdType.MESH
F32 = jnp.float32
BF16 = jnp.bfloat16
NN = (((1,), (0,)), ((), ()))
NT = (((1,), (1,)), ((), ()))
QUAD = 4


def mm(a, b, dims=NN):
    return lax.dot_general(a, b, dims, preferred_element_type=F32)


def flip(a):
    return jnp.transpose(a.astype(F32)).astype(a.dtype)


def one_minus_exp(y):
    z = y * 0.125
    f = z * (1.0 + z * (1 / 2) * (1.0 + z * (1 / 3) * (1.0 + z * (1 / 4) * (1.0 + z * (1 / 5) * (1.0 + z * (1 / 6) * (1.0 + z * (1 / 7)))))))
    for _ in range(3):
        f = f * (f + 2.0)
    return -f


def partner(place, j):
    out, bit = place, 1
    while bit <= j:
        if j & bit:
            out = out + bit - 2 * bit * lax.rem(place // bit, 2)
        bit *= 2
    return out


def body(line, total_rows, head_count, x_hbm, lr_hbm, g_hbm, w_hbm, gf_ref, gw_ref,
         x_ref, lr_ref, g_ref, w_ref, w_other, xr, xs, xw, gs, xw_far, gs_far, bt, gx, bc_all,
         pm, acc, z_send, z_recv, full,
         in_sem, w_sem, e_sem_s, e_sem_r, x_sem_s, x_sem_r, o_sem, b_sem_s, b_sem_r,
         z_sem_s, z_sem_r, agz_sem_s, agz_sem_r, ag_sem_s, ag_sem_r, m_sem_s, m_sem_r):
    rows, width = x_ref.shape
    shard = w_ref.shape[0]
    state = w_ref.shape[1] // 2
    inv_root = state ** (-0.5)
    dp = lax.axis_index("dp")
    ctx = lax.axis_index("ctx")
    place = lax.rem(dp, QUAD)
    spot = dp // QUAD
    blocks = acc.shape[0]
    per_shard = blocks // 2
    mate = {"ctx": 1 - ctx}
    far_first = (3, 2, 1)
    hubs = [{"dp": spot * QUAD + partner(place, j), "ctx": 1} for j in range(1, QUAD)]
    leaves = [{"dp": spot * QUAD + partner(place, j), "ctx": 0} for j in range(1, QUAD)]
    if line == blocks:
        lines = [{"dp": partner(spot, j) * QUAD + place} for j in range(1, line)]
    else:
        lines = []
        m = 1
        while m < line:
            lines.append({"dp": dp + QUAD * m * (1 - 2 * lax.rem(spot // m, 2))})
            m *= 2

    def remote(src, dst, s_sem, r_sem, who):
        return pltpu.make_async_remote_copy(
            src_ref=src, dst_ref=dst, send_sem=s_sem, recv_sem=r_sem, device_id=who, device_id_type=MESH)

    def send(src, dst, s_sem, r_sem, who):
        copy = remote(src, dst, s_sem, r_sem, who)
        copy.start()
        return copy

    barrier = pltpu.get_barrier_semaphore()

    @pl.when(ctx == 1)
    def _():
        for who in hubs + leaves + lines:
            pl.semaphore_signal(barrier, inc=1, device_id=who, device_id_type=MESH)

    pl.semaphore_signal(barrier, inc=1, device_id=mate, device_id_type=MESH)

    loads = [pltpu.make_async_copy(a, b, in_sem.at[k])
             for k, (a, b) in enumerate(((x_hbm, x_ref), (lr_hbm, lr_ref), (w_hbm, w_ref), (g_hbm, g_ref)))]
    for load in loads:
        load.start()

    own = pl.ds(pl.multiple_of(ctx * shard, shard), shard)
    far = pl.ds(pl.multiple_of((1 - ctx) * shard, shard), shard)

    quarter = shard // QUAD

    def columns(c, q):
        return pl.ds(pl.multiple_of(c * shard + q * quarter, quarter), quarter)

    def band(k):
        return pl.ds(pl.multiple_of(k * rows, rows), rows)

    pl.semaphore_wait(barrier, QUAD + ctx * len(lines))
    w_copy = send(w_hbm, w_other, w_sem.at[0], w_sem.at[1], mate)

    def x_copy(j, c, source, who):
        return remote(x_ref.at[:, columns(c, partner(place, j))], xr.at[j, c, band(source)],
                      x_sem_s.at[j, c], x_sem_r.at[j, source, c], who)

    loads[0].wait()
    x_copies = [x_copy(j, c, ctx, hubs[j - 1]) for j, c in ((3, 0), (3, 1), (1, 0), (2, 0), (1, 1), (2, 1))]
    for copy in x_copies:
        copy.start()
    own_copies = [pltpu.make_async_copy(x_ref.at[:, columns(c, place)], xr.at[0, c, band(ctx)], o_sem.at[c])
                  for c in range(2)]
    mate_copies = [x_copy(0, c, 0, mate) for c in range(2)]

    @pl.when(ctx == 1)
    def _():
        for copy in own_copies:
            copy.start()

    @pl.when(ctx == 0)
    def _():
        for copy in mate_copies:
            copy.start()

    ti = lax.broadcasted_iota(jnp.int32, (rows, rows), 0)
    si = lax.broadcasted_iota(jnp.int32, (rows, rows), 1)
    tri = jnp.where(ti <= si, 1.0, 0.0).astype(F32)
    hi_ = lax.broadcasted_iota(jnp.int32, (rows, width), 0)
    ci_ = lax.broadcasted_iota(jnp.int32, (rows, width), 1)
    head_dim = width // head_count
    lo_c = hi_ * head_dim
    spread = jnp.where((ci_ >= lo_c) & (ci_ < lo_c + head_dim), 1.0, 0.0).astype(BF16)

    loads[1].wait()
    lr = lr_ref[...]
    lr_t = jnp.concatenate([lr, jnp.zeros((rows - head_count, rows), F32)], axis=0)
    incl_t = lax.dot_general(lr_t, tri, NN, precision=lax.Precision.HIGHEST, preferred_element_type=F32)
    excl_t = incl_t - lr_t
    lr_pad = jnp.transpose(lr_t)
    incl = jnp.transpose(incl_t)
    excl = incl - lr_pad
    total = incl[rows - 1:rows, :]
    step = jnp.sqrt(one_minus_exp(2.0 * lr_pad))
    first = ctx == 0
    rate_x = jnp.exp(jnp.where(first, total - incl, excl))
    rate_g = jnp.exp(jnp.where(first, total - excl, incl)) * inv_root

    def widen(v):
        top = v.astype(BF16)
        low = (v - top.astype(F32)).astype(BF16)
        return mm(top, spread) + mm(low, spread)

    step_w = widen(step)
    gx[...] = step_w
    wide_x = widen(rate_x * step)
    loads[2].wait()
    xf = x_ref[...].astype(F32)
    xw[...] = (xf * wide_x).astype(BF16)
    e_copies = [send(xw, xw_far, e_sem_s.at[0], e_sem_r.at[0], mate)]
    loads[3].wait()
    gs[...] = (g_ref[...].astype(F32) * widen(rate_g)).astype(BF16)
    e_copies.append(send(gs, gs_far, e_sem_s.at[1], e_sem_r.at[1], mate))

    bc = mm(x_ref[:, own], w_ref[...])
    w_copy.wait()
    bc = (bc + mm(x_ref[:, far], w_other[...])).astype(BF16)
    b_in = bc[:, :state]
    c_out = bc[:, state:]

    bt[:, :rows] = jnp.concatenate([flip(b_in), flip(c_out)], axis=0)
    e_copies.append(send(bt.at[:, slice(0, rows)], bt.at[:, slice(rows, 2 * rows)],
                         e_sem_s.at[2], e_sem_r.at[2], mate))
    xs[...] = (x_ref[...].astype(F32) * gx[...]).astype(BF16)

    twice = jnp.where(ti == si, 2.0, 1.0).astype(F32)
    dots = mm(b_in, c_out, NT) * (twice * inv_root)
    upper = si >= ti
    lane = lax.broadcasted_iota(jnp.int32, (rows, 2 * head_dim), 1)

    def apart(cols):
        gp = g_ref[:, cols]
        zero = jnp.zeros_like(gp)
        return jnp.concatenate([jnp.where(lane < head_dim, gp, zero), jnp.where(lane < head_dim, zero, gp)], axis=0)

    wb = jnp.zeros((rows, rows), F32)
    for pair in range(head_count // 2):
        cols = slice(pair * 2 * head_dim, (pair + 1) * 2 * head_dim)
        cross = mm(xs[:, cols], apart(cols), NT)
        for j in range(2):
            h = 2 * pair + j
            gap = jnp.where(upper, incl_t[h:h + 1, :] - incl[:, h:h + 1], excl[:, h:h + 1] - excl_t[h:h + 1, :])
            mix = jnp.exp(gap)
            wb = wb + mix * cross[:, j * rows:(j + 1) * rows]
            pm[pair, :, j * rows:(j + 1) * rows] = (mix * dots).astype(BF16)
    wb = (wb * (twice * inv_root)).astype(BF16)
    e_copies[0].wait_recv()
    far_c = mm(xw_far[...], gs[...], NT).astype(BF16)
    e_copies[1].wait_recv()
    far_b = mm(xw[...], gs_far[...], NT).astype(BF16)
    e_copies[2].wait_recv()
    grad_b = mm(bt[state:, :], jnp.concatenate([wb, far_b], axis=1), NT)
    grad_c = mm(bt[:state, :], jnp.concatenate([wb, far_c], axis=0))
    grad_bc = jnp.concatenate([grad_b, grad_c], axis=0).astype(BF16)
    bc_all[0, :, band(ctx)] = grad_bc

    def b_copy(j, source, who):
        return remote(bc_all.at[0, :, band(source)], bc_all.at[j, :, band(source)],
                      b_sem_s.at[j], b_sem_r.at[j, source], who)

    b_copies = [b_copy(j, ctx, hubs[j - 1]) for j in far_first]
    for copy in b_copies:
        copy.start()
    mate_copies.append(b_copy(0, 0, mate))

    @pl.when(ctx == 0)
    def _():
        mate_copies[2].start()

    def finish_features():
        for pair in range(head_count // 2):
            cols = slice(pair * 2 * head_dim, (pair + 1) * 2 * head_dim)
            gx[:, cols] = gx[:, cols] * mm(pm[pair], apart(cols))
        gx[...] = mm(mm(b_in, bt[state:, rows:]).astype(BF16), gs_far[...]) * wide_x + gx[...]
        left = flip(grad_bc)
        gf_ref[:, own] = (gx[:, own] + mm(left, w_ref[...], NT)).astype(BF16)
        gf_ref[:, far] = (gx[:, far] + mm(left, w_other[...], NT)).astype(BF16)

    finish_features()

    scale = total_rows ** (-0.5)
    parts = 2
    h = 2 * state // parts
    parts_of = [slice(p * h, (p + 1) * h) for p in range(parts)]
    size = acc.shape[2]

    def gather_copy(j, t, p, k):
        return remote(full.at[j, :, parts_of[p]], gw_ref.at[place, lax.rem(t, per_shard), :, parts_of[p]],
                      ag_sem_s.at[j, k - 1, p], ag_sem_r.at[k - 1, lax.rem(t, per_shard), p],
                      {"dp": spot * QUAD + partner(place, k), "ctx": t // per_shard})

    def mate_copy(j, t, p):
        return remote(full.at[j, :, parts_of[p]], gw_ref.at[place, lax.rem(t, per_shard), :, parts_of[p]],
                      m_sem_s.at[j, p], m_sem_r.at[lax.rem(t, per_shard), p], {"ctx": 0})

    def spread_out(j, t, p):
        for k in far_first:
            gather_copy(j, t, p, k).start()

        @pl.when(t < per_shard)
        def _():
            mate_copy(j, t, p).start()

        @pl.when(t >= per_shard)
        def _():
            gw_ref[place, lax.rem(t, per_shard), :, parts_of[p]] = full[j, :, parts_of[p]]

    def turned(v):
        return jnp.transpose(v * scale).astype(BF16)

    @pl.when(ctx == 1)
    def _():
        for copy in own_copies:
            copy.wait()
        for c in range(2):
            mate_copies[c].wait_recv()
        mate_copies[2].wait_recv()
        for j in far_first:
            for source in range(2):
                for c in range(2):
                    x_copy(j, c, source, hubs[j - 1]).wait_recv()
        total_t = [mm(bc_all[0], xr[0, c]) for c in range(2)]
        for j in far_first:
            for source in range(2):
                b_copy(j, source, hubs[j - 1]).wait_recv()
        for j in far_first:
            total_t = [total_t[c] + mm(bc_all[j], xr[j, c]) for c in range(2)]
        for t in range(blocks):
            i = t % per_shard
            acc[t] = total_t[t // per_shard][:, i * size:(i + 1) * size]

        if line == blocks:
            order = range(1, line)
            owner = [partner(spot, j) for j in range(line)]

            def z_copy(j, p):
                return remote(z_send.at[j - 1, 0, parts_of[p]], z_recv.at[j - 1, 0, parts_of[p]],
                              z_sem_s.at[j - 1, p], z_sem_r.at[j - 1, p], lines[j - 1])

            def along(j, p):
                return remote(full.at[0, :, parts_of[p]], full.at[j, :, parts_of[p]],
                              agz_sem_s.at[j - 1, p], agz_sem_r.at[j - 1, p], lines[j - 1])

            for p in range(parts):
                for j in reversed(order):
                    z_send[j - 1, 0, parts_of[p]] = acc[owner[j], parts_of[p]].astype(BF16)
                    z_copy(j, p).start()
            for p in range(parts):
                whole = acc[spot, parts_of[p]]
                for j in order:
                    z_copy(j, p).wait_recv()
                    whole = whole + z_recv[j - 1, 0, parts_of[p]].astype(F32)
                full[0, :, parts_of[p]] = turned(whole)
                for j in order:
                    along(j, p).start()
                spread_out(0, spot, p)
            for p in range(parts):
                for j in order:
                    along(j, p).wait_recv()
                    spread_out(j, owner[j], p)
            for p in range(parts):
                for j in order:
                    z_copy(j, p).wait_send()
                    along(j, p).wait_send()
        else:
            owner = [jnp.int32(t) for t in range(blocks)]
            for k in range(len(lines)):
                z_send[k] = acc[...].astype(BF16)
                copy = send(z_send.at[k], z_recv.at[k], z_sem_s.at[k, 0], z_sem_r.at[k, 0], lines[k])
                copy.wait()
                acc[...] = z_send[k].astype(F32) + z_recv[k].astype(F32)
            for t in range(blocks):
                for p in range(parts):
                    full[t, :, parts_of[p]] = turned(acc[t, parts_of[p]])
                    spread_out(t, owner[t], p)
        for j in range(blocks):
            for p in range(parts):
                for k in far_first:
                    gather_copy(j, owner[j], p, k).wait_send()

                @pl.when(owner[j] < per_shard)
                def _():
                    mate_copy(j, owner[j], p).wait_send()

    for k in far_first:
        for i in range(per_shard):
            for p in range(parts):
                gather_copy(0, i, p, k).wait_recv()
    for copy in x_copies + b_copies + e_copies:
        copy.wait_send()

    @pl.when(ctx == 0)
    def _():
        for copy in mate_copies:
            copy.wait_send()
        for i in range(per_shard):
            for p in range(parts):
                mate_copy(0, i, p).wait_recv()


def deliver(gf_ref, gw_ref, gf_hbm, gw_hbm, sem):
    copies = [pltpu.make_async_copy(a, b, sem.at[k]) for k, (a, b) in enumerate(((gf_ref, gf_hbm), (gw_ref, gw_hbm)))]
    for copy in copies:
        copy.start()
    for copy in copies:
        copy.wait()


def per_device(dp_count, ctx_count, features, log_decays, cotangent, bc_weight):
    x, lr, g = features[0], jnp.swapaxes(log_decays[0], 0, 1), cotangent[0]
    rows, width = x.shape
    shard, cols = bc_weight.shape
    total_rows = features.shape[0] * dp_count * rows * ctx_count
    head_count = lr.shape[0]
    line = dp_count // QUAD
    quarter = shard // QUAD
    size = 128
    blocks = 2 * quarter // size
    direct = line == blocks
    hops = max(line - 1 if direct else line.bit_length() - 1, 1)
    deep = 1 if direct else blocks
    dma = pltpu.SemaphoreType.DMA
    vm = pl.BlockSpec(memory_space=pltpu.VMEM)
    gf, gw = pl.pallas_call(
        functools.partial(body, line, total_rows, head_count),
        out_shape=(pltpu.VMEM((rows, width), BF16), pltpu.VMEM((QUAD, blocks // 2, size, cols), BF16)),
        in_specs=[pl.BlockSpec(memory_space=pltpu.HBM)] * 4,
        out_specs=(vm, vm),
        scratch_shapes=[
            pltpu.VMEM((rows, width), BF16),
            pltpu.VMEM((head_count, rows), F32),
            pltpu.VMEM((rows, width), BF16),
            pltpu.VMEM((shard, cols), BF16),
            pltpu.VMEM((shard, cols), BF16),
            pltpu.VMEM((QUAD, 2, 2 * rows, quarter), BF16),
            pltpu.VMEM((rows, width), BF16),
            pltpu.VMEM((rows, width), BF16),
            pltpu.VMEM((rows, width), BF16),
            pltpu.VMEM((rows, width), BF16),
            pltpu.VMEM((rows, width), BF16),
            pltpu.VMEM((cols, 2 * rows), BF16),
            pltpu.VMEM((rows, width), F32),
            pltpu.VMEM((QUAD, cols, 2 * rows), BF16),
            pltpu.VMEM((head_count // 2, rows, 2 * rows), BF16),
            pltpu.VMEM((blocks, cols, size), F32),
            pltpu.VMEM((hops, deep, cols, size), BF16),
            pltpu.VMEM((hops, deep, cols, size), BF16),
            pltpu.VMEM((blocks, size, cols), BF16),
            dma((4,)), dma((2,)), dma((3,)), dma((3,)),
            dma((QUAD, 2)), dma((QUAD, 2, 2)), dma((2,)), dma((QUAD,)), dma((QUAD, 2)),
            dma((hops, 2)), dma((hops, 2)), dma((hops, 2)), dma((hops, 2)),
            dma((blocks, QUAD - 1, 2)), dma((QUAD - 1, blocks // 2, 2)), dma((blocks, 2)), dma((blocks // 2, 2)),
        ],
        compiler_params=pltpu.CompilerParams(
            collective_id=0, has_side_effects=True, vmem_limit_bytes=64256 * 1024),
    )(x, lr, g, bc_weight)
    gw = gw.reshape(shard, cols)
    hbm = pl.BlockSpec(memory_space=pltpu.HBM)
    gf, gw = pl.pallas_call(
        deliver,
        out_shape=(jax.ShapeDtypeStruct((rows, width), BF16), jax.ShapeDtypeStruct((shard, cols), BF16)),
        in_specs=[vm, vm],
        out_specs=(hbm, hbm),
        scratch_shapes=[dma((2,))],
        compiler_params=pltpu.CompilerParams(vmem_limit_bytes=2 * 2**20),
    )(gf, gw)
    return gf[None], gw


def solution(mesh):
    placed = (P("dp", "ctx", None), P("dp", "ctx", None), P("dp", "ctx", None), P("ctx", None))
    return jax.shard_map(
        functools.partial(per_device, mesh.shape["dp"], mesh.shape["ctx"]),
        mesh=mesh,
        in_specs=placed,
        out_specs=(P("dp", "ctx", None), P("ctx", None)),
        check_vma=False,
    )
```

```python
import functools

import jax
import jax.numpy as jnp
from jax import lax
from jax.experimental import pallas as pl
from jax.experimental.pallas import tpu as pltpu
from jax.sharding import PartitionSpec as P

MESH = pl.DeviceIdType.MESH
F32 = jnp.float32
BF16 = jnp.bfloat16
NN = (((1,), (0,)), ((), ()))
NT = (((1,), (1,)), ((), ()))
QUAD = 4


def mm(a, b, dims=NN):
    return lax.dot_general(a, b, dims, preferred_element_type=F32)


def flip(a):
    return jnp.transpose(a.astype(F32)).astype(a.dtype)


def one_minus_exp(y):
    z = y * 0.125
    f = z * (1.0 + z * (1 / 2) * (1.0 + z * (1 / 3) * (1.0 + z * (1 / 4) * (1.0 + z * (1 / 5) * (1.0 + z * (1 / 6) * (1.0 + z * (1 / 7)))))))
    for _ in range(3):
        f = f * (f + 2.0)
    return -f


def partner(place, j):
    out, bit = place, 1
    while bit <= j:
        if j & bit:
            out = out + bit - 2 * bit * lax.rem(place // bit, 2)
        bit *= 2
    return out


def body(line, total_rows, head_count, x_hbm, lr_hbm, g_hbm, w_hbm, gf_ref, gw_ref,
         x_ref, lr_ref, g_ref, w_ref, w_other, xr, xs, xw, gs, xw_far, gs_far, bt, gx, bc_all,
         pm, acc, z_send, z_recv, full,
         in_sem, w_sem, e_sem_s, e_sem_r, x_sem_s, x_sem_r, o_sem, b_sem_s, b_sem_r,
         z_sem_s, z_sem_r, agz_sem_s, agz_sem_r, ag_sem_s, ag_sem_r, m_sem_s, m_sem_r):
    rows, width = x_ref.shape
    shard = w_ref.shape[0]
    state = w_ref.shape[1] // 2
    inv_root = state ** (-0.5)
    dp = lax.axis_index("dp")
    ctx = lax.axis_index("ctx")
    place = lax.rem(dp, QUAD)
    spot = dp // QUAD
    blocks = acc.shape[0]
    per_shard = blocks // 2
    mate = {"ctx": 1 - ctx}
    far_first = (3, 2, 1)
    hubs = [{"dp": spot * QUAD + partner(place, j), "ctx": 1} for j in range(1, QUAD)]
    leaves = [{"dp": spot * QUAD + partner(place, j), "ctx": 0} for j in range(1, QUAD)]
    if line == blocks:
        lines = [{"dp": partner(spot, j) * QUAD + place} for j in range(1, line)]
    else:
        lines = []
        m = 1
        while m < line:
            lines.append({"dp": dp + QUAD * m * (1 - 2 * lax.rem(spot // m, 2))})
            m *= 2

    def remote(src, dst, s_sem, r_sem, who):
        return pltpu.make_async_remote_copy(
            src_ref=src, dst_ref=dst, send_sem=s_sem, recv_sem=r_sem, device_id=who, device_id_type=MESH)

    def send(src, dst, s_sem, r_sem, who):
        copy = remote(src, dst, s_sem, r_sem, who)
        copy.start()
        return copy

    barrier = pltpu.get_barrier_semaphore()

    @pl.when(ctx == 1)
    def _():
        for who in hubs + leaves + lines:
            pl.semaphore_signal(barrier, inc=1, device_id=who, device_id_type=MESH)

    pl.semaphore_signal(barrier, inc=1, device_id=mate, device_id_type=MESH)

    loads = [pltpu.make_async_copy(a, b, in_sem.at[k])
             for k, (a, b) in enumerate(((x_hbm, x_ref), (lr_hbm, lr_ref), (w_hbm, w_ref), (g_hbm, g_ref)))]
    for load in loads:
        load.start()

    own = pl.ds(pl.multiple_of(ctx * shard, shard), shard)
    far = pl.ds(pl.multiple_of((1 - ctx) * shard, shard), shard)

    quarter = shard // QUAD

    def columns(c, q):
        return pl.ds(pl.multiple_of(c * shard + q * quarter, quarter), quarter)

    def band(k):
        return pl.ds(pl.multiple_of(k * rows, rows), rows)

    pl.semaphore_wait(barrier, QUAD + ctx * len(lines))
    w_copy = send(w_hbm, w_other, w_sem.at[0], w_sem.at[1], mate)

    def x_copy(j, c, source, who):
        return remote(x_ref.at[:, columns(c, partner(place, j))], xr.at[j, c, band(source)],
                      x_sem_s.at[j, c], x_sem_r.at[j, source, c], who)

    loads[0].wait()
    x_copies = [x_copy(j, c, ctx, hubs[j - 1]) for j, c in ((3, 0), (3, 1), (1, 0), (2, 0), (1, 1), (2, 1))]
    for copy in x_copies:
        copy.start()
    own_copies = [pltpu.make_async_copy(x_ref.at[:, columns(c, place)], xr.at[0, c, band(ctx)], o_sem.at[c])
                  for c in range(2)]
    mate_copies = [x_copy(0, c, 0, mate) for c in range(2)]

    @pl.when(ctx == 1)
    def _():
        for copy in own_copies:
            copy.start()

    @pl.when(ctx == 0)
    def _():
        for copy in mate_copies:
            copy.start()

    ti = lax.broadcasted_iota(jnp.int32, (rows, rows), 0)
    si = lax.broadcasted_iota(jnp.int32, (rows, rows), 1)
    tri = jnp.where(ti <= si, 1.0, 0.0).astype(F32)
    hi_ = lax.broadcasted_iota(jnp.int32, (rows, width), 0)
    ci_ = lax.broadcasted_iota(jnp.int32, (rows, width), 1)
    head_dim = width // head_count
    lo_c = hi_ * head_dim
    spread = jnp.where((ci_ >= lo_c) & (ci_ < lo_c + head_dim), 1.0, 0.0).astype(BF16)

    loads[1].wait()
    lr = lr_ref[...]
    lr_t = jnp.concatenate([lr, jnp.zeros((rows - head_count, rows), F32)], axis=0)
    incl_t = lax.dot_general(lr_t, tri, NN, precision=lax.Precision.HIGHEST, preferred_element_type=F32)
    excl_t = incl_t - lr_t
    lr_pad = jnp.transpose(lr_t)
    incl = jnp.transpose(incl_t)
    excl = incl - lr_pad
    total = incl[rows - 1:rows, :]
    step = jnp.sqrt(one_minus_exp(2.0 * lr_pad))
    first = ctx == 0
    rate_x = jnp.exp(jnp.where(first, total - incl, excl))
    rate_g = jnp.exp(jnp.where(first, total - excl, incl)) * inv_root

    def widen(v):
        top = v.astype(BF16)
        low = (v - top.astype(F32)).astype(BF16)
        return mm(top, spread) + mm(low, spread)

    step_w = widen(step)
    gx[...] = step_w
    wide_x = widen(rate_x * step)
    loads[2].wait()
    xf = x_ref[...].astype(F32)
    xw[...] = (xf * wide_x).astype(BF16)
    e_copies = [send(xw, xw_far, e_sem_s.at[0], e_sem_r.at[0], mate)]
    loads[3].wait()
    gs[...] = (g_ref[...].astype(F32) * widen(rate_g)).astype(BF16)
    e_copies.append(send(gs, gs_far, e_sem_s.at[1], e_sem_r.at[1], mate))

    bc = mm(x_ref[:, own], w_ref[...])
    w_copy.wait()
    bc = (bc + mm(x_ref[:, far], w_other[...])).astype(BF16)
    b_in = bc[:, :state]
    c_out = bc[:, state:]

    bt[:, :rows] = jnp.concatenate([flip(b_in), flip(c_out)], axis=0)
    e_copies.append(send(bt.at[:, slice(0, rows)], bt.at[:, slice(rows, 2 * rows)],
                         e_sem_s.at[2], e_sem_r.at[2], mate))
    xs[...] = (x_ref[...].astype(F32) * gx[...]).astype(BF16)

    twice = jnp.where(ti == si, 2.0, 1.0).astype(F32)
    dots = mm(b_in, c_out, NT) * (twice * inv_root)
    upper = si >= ti
    lane = lax.broadcasted_iota(jnp.int32, (rows, 2 * head_dim), 1)

    def apart(cols):
        gp = g_ref[:, cols]
        zero = jnp.zeros_like(gp)
        return jnp.concatenate([jnp.where(lane < head_dim, gp, zero), jnp.where(lane < head_dim, zero, gp)], axis=0)

    wb = jnp.zeros((rows, rows), F32)
    for pair in range(head_count // 2):
        cols = slice(pair * 2 * head_dim, (pair + 1) * 2 * head_dim)
        cross = mm(xs[:, cols], apart(cols), NT)
        for j in range(2):
            h = 2 * pair + j
            gap = jnp.where(upper, incl_t[h:h + 1, :] - incl[:, h:h + 1], excl[:, h:h + 1] - excl_t[h:h + 1, :])
            mix = jnp.exp(gap)
            wb = wb + mix * cross[:, j * rows:(j + 1) * rows]
            pm[pair, :, j * rows:(j + 1) * rows] = (mix * dots).astype(BF16)
    wb = (wb * (twice * inv_root)).astype(BF16)
    e_copies[0].wait_recv()
    far_c = mm(xw_far[...], gs[...], NT).astype(BF16)
    e_copies[1].wait_recv()
    far_b = mm(xw[...], gs_far[...], NT).astype(BF16)
    e_copies[2].wait_recv()
    grad_b = mm(bt[state:, :], jnp.concatenate([wb, far_b], axis=1), NT)
    grad_c = mm(bt[:state, :], jnp.concatenate([wb, far_c], axis=0))
    grad_bc = jnp.concatenate([grad_b, grad_c], axis=0).astype(BF16)
    bc_all[0, :, band(ctx)] = grad_bc

    def b_copy(j, source, who):
        return remote(bc_all.at[0, :, band(source)], bc_all.at[j, :, band(source)],
                      b_sem_s.at[j], b_sem_r.at[j, source], who)

    b_copies = [b_copy(j, ctx, hubs[j - 1]) for j in far_first]
    for copy in b_copies:
        copy.start()
    mate_copies.append(b_copy(0, 0, mate))

    @pl.when(ctx == 0)
    def _():
        mate_copies[2].start()

    def finish_features():
        for pair in range(head_count // 2):
            cols = slice(pair * 2 * head_dim, (pair + 1) * 2 * head_dim)
            gx[:, cols] = gx[:, cols] * mm(pm[pair], apart(cols))
        gx[...] = mm(mm(b_in, bt[state:, rows:]).astype(BF16), gs_far[...]) * wide_x + gx[...]
        left = flip(grad_bc)
        gf_ref[:, own] = (gx[:, own] + mm(left, w_ref[...], NT)).astype(BF16)
        gf_ref[:, far] = (gx[:, far] + mm(left, w_other[...], NT)).astype(BF16)

    finish_features()

    scale = total_rows ** (-0.5)
    parts = 2
    h = 2 * state // parts
    parts_of = [slice(p * h, (p + 1) * h) for p in range(parts)]
    size = acc.shape[2]

    def gather_copy(j, t, p, k):
        return remote(full.at[j, :, parts_of[p]], gw_ref.at[place, lax.rem(t, per_shard), :, parts_of[p]],
                      ag_sem_s.at[j, k - 1, p], ag_sem_r.at[k - 1, lax.rem(t, per_shard), p],
                      {"dp": spot * QUAD + partner(place, k), "ctx": t // per_shard})

    def mate_copy(j, t, p):
        return remote(full.at[j, :, parts_of[p]], gw_ref.at[place, lax.rem(t, per_shard), :, parts_of[p]],
                      m_sem_s.at[j, p], m_sem_r.at[lax.rem(t, per_shard), p], mate)

    def spread_out(me, j, t, p):
        for k in far_first:
            gather_copy(j, t, p, k).start()

        @pl.when(t // per_shard != me)
        def _():
            mate_copy(j, t, p).start()

        @pl.when(t // per_shard == me)
        def _():
            gw_ref[place, lax.rem(t, per_shard), :, parts_of[p]] = full[j, :, parts_of[p]]

    def settle(me, j, t, p):
        for k in far_first:
            gather_copy(j, t, p, k).wait_send()

        @pl.when(t // per_shard != me)
        def _():
            mate_copy(j, t, p).wait_send()

    if line == blocks:
        owner = [partner(spot, j) for j in range(line)]
        handler = (1, 0, 1, 1)
    else:
        owner = [jnp.int32(t) for t in range(blocks)]
        handler = (1,) * blocks

    def along(j, p):
        return remote(full.at[0, :, parts_of[p]], full.at[j, :, parts_of[p]],
                      agz_sem_s.at[j - 1, p], agz_sem_r.at[j - 1, p], {**lines[j - 1], "ctx": handler[j]})

    def turned(v):
        return jnp.transpose(v * scale).astype(BF16)

    @pl.when(ctx == 1)
    def _():
        for copy in own_copies:
            copy.wait()
        for c in range(2):
            mate_copies[c].wait_recv()
        mate_copies[2].wait_recv()
        for j in far_first:
            for source in range(2):
                for c in range(2):
                    x_copy(j, c, source, hubs[j - 1]).wait_recv()
        total_t = [mm(bc_all[0], xr[0, c]) for c in range(2)]
        for j in far_first:
            for source in range(2):
                b_copy(j, source, hubs[j - 1]).wait_recv()
        for j in far_first:
            total_t = [total_t[c] + mm(bc_all[j], xr[j, c]) for c in range(2)]
        for t in range(blocks):
            i = t % per_shard
            acc[t] = total_t[t // per_shard][:, i * size:(i + 1) * size]

        if line == blocks:
            order = range(1, line)

            def z_copy(j, p):
                return remote(z_send.at[j - 1, 0, parts_of[p]], z_recv.at[j - 1, 0, parts_of[p]],
                              z_sem_s.at[j - 1, p], z_sem_r.at[j - 1, p], lines[j - 1])

            for p in range(parts):
                for j in reversed(order):
                    z_send[j - 1, 0, parts_of[p]] = acc[owner[j], parts_of[p]].astype(BF16)
                    z_copy(j, p).start()
            for p in range(parts):
                whole = acc[spot, parts_of[p]]
                for j in order:
                    z_copy(j, p).wait_recv()
                    whole = whole + z_recv[j - 1, 0, parts_of[p]].astype(F32)
                full[0, :, parts_of[p]] = turned(whole)
                for j in order:
                    along(j, p).start()
                spread_out(1, 0, spot, p)
            for p in range(parts):
                for j in order:
                    if handler[j] == 1:
                        along(j, p).wait_recv()
                        spread_out(1, j, owner[j], p)
            for p in range(parts):
                for j in order:
                    z_copy(j, p).wait_send()
                    along(j, p).wait_send()
        else:
            for k in range(len(lines)):
                z_send[k] = acc[...].astype(BF16)
                copy = send(z_send.at[k], z_recv.at[k], z_sem_s.at[k, 0], z_sem_r.at[k, 0], lines[k])
                copy.wait()
                acc[...] = z_send[k].astype(F32) + z_recv[k].astype(F32)
            for t in range(blocks):
                for p in range(parts):
                    full[t, :, parts_of[p]] = turned(acc[t, parts_of[p]])
                    spread_out(1, t, owner[t], p)
        for j in range(blocks):
            for p in range(parts):
                if handler[j] == 1:
                    settle(1, j, owner[j], p)
                else:
                    @pl.when(owner[j] // per_shard == 1)
                    def _():
                        mate_copy(j, owner[j], p).wait_recv()

    @pl.when(ctx == 0)
    def _():
        for p in range(parts):
            for j in range(blocks):
                if handler[j] == 0:
                    along(j, p).wait_recv()
                    spread_out(0, j, owner[j], p)
        for j in range(blocks):
            for p in range(parts):
                if handler[j] == 0:
                    settle(0, j, owner[j], p)
                else:
                    @pl.when(owner[j] // per_shard == 0)
                    def _():
                        mate_copy(j, owner[j], p).wait_recv()

    for k in far_first:
        for i in range(per_shard):
            for p in range(parts):
                gather_copy(0, i, p, k).wait_recv()
    for copy in x_copies + b_copies + e_copies:
        copy.wait_send()

    @pl.when(ctx == 0)
    def _():
        for copy in mate_copies:
            copy.wait_send()


def deliver(gf_ref, gw_ref, gf_hbm, gw_hbm, sem):
    copies = [pltpu.make_async_copy(a, b, sem.at[k]) for k, (a, b) in enumerate(((gf_ref, gf_hbm), (gw_ref, gw_hbm)))]
    for copy in copies:
        copy.start()
    for copy in copies:
        copy.wait()


def per_device(dp_count, ctx_count, features, log_decays, cotangent, bc_weight):
    x, lr, g = features[0], jnp.swapaxes(log_decays[0], 0, 1), cotangent[0]
    rows, width = x.shape
    shard, cols = bc_weight.shape
    total_rows = features.shape[0] * dp_count * rows * ctx_count
    head_count = lr.shape[0]
    line = dp_count // QUAD
    quarter = shard // QUAD
    size = 128
    blocks = 2 * quarter // size
    direct = line == blocks
    hops = max(line - 1 if direct else line.bit_length() - 1, 1)
    deep = 1 if direct else blocks
    dma = pltpu.SemaphoreType.DMA
    vm = pl.BlockSpec(memory_space=pltpu.VMEM)
    gf, gw = pl.pallas_call(
        functools.partial(body, line, total_rows, head_count),
        out_shape=(pltpu.VMEM((rows, width), BF16), pltpu.VMEM((QUAD, blocks // 2, size, cols), BF16)),
        in_specs=[pl.BlockSpec(memory_space=pltpu.HBM)] * 4,
        out_specs=(vm, vm),
        scratch_shapes=[
            pltpu.VMEM((rows, width), BF16),
            pltpu.VMEM((head_count, rows), F32),
            pltpu.VMEM((rows, width), BF16),
            pltpu.VMEM((shard, cols), BF16),
            pltpu.VMEM((shard, cols), BF16),
            pltpu.VMEM((QUAD, 2, 2 * rows, quarter), BF16),
            pltpu.VMEM((rows, width), BF16),
            pltpu.VMEM((rows, width), BF16),
            pltpu.VMEM((rows, width), BF16),
            pltpu.VMEM((rows, width), BF16),
            pltpu.VMEM((rows, width), BF16),
            pltpu.VMEM((cols, 2 * rows), BF16),
            pltpu.VMEM((rows, width), F32),
            pltpu.VMEM((QUAD, cols, 2 * rows), BF16),
            pltpu.VMEM((head_count // 2, rows, 2 * rows), BF16),
            pltpu.VMEM((blocks, cols, size), F32),
            pltpu.VMEM((hops, deep, cols, size), BF16),
            pltpu.VMEM((hops, deep, cols, size), BF16),
            pltpu.VMEM((blocks, size, cols), BF16),
            dma((4,)), dma((2,)), dma((3,)), dma((3,)),
            dma((QUAD, 2)), dma((QUAD, 2, 2)), dma((2,)), dma((QUAD,)), dma((QUAD, 2)),
            dma((hops, 2)), dma((hops, 2)), dma((hops, 2)), dma((hops, 2)),
            dma((blocks, QUAD - 1, 2)), dma((QUAD - 1, blocks // 2, 2)), dma((blocks, 2)), dma((blocks // 2, 2)),
        ],
        compiler_params=pltpu.CompilerParams(
            collective_id=0, has_side_effects=True, vmem_limit_bytes=64256 * 1024),
    )(x, lr, g, bc_weight)
    gw = gw.reshape(shard, cols)
    hbm = pl.BlockSpec(memory_space=pltpu.HBM)
    gf, gw = pl.pallas_call(
        deliver,
        out_shape=(jax.ShapeDtypeStruct((rows, width), BF16), jax.ShapeDtypeStruct((shard, cols), BF16)),
        in_specs=[vm, vm],
        out_specs=(hbm, hbm),
        scratch_shapes=[dma((2,))],
        compiler_params=pltpu.CompilerParams(vmem_limit_bytes=2 * 2**20),
    )(gf, gw)
    return gf[None], gw


def solution(mesh):
    placed = (P("dp", "ctx", None), P("dp", "ctx", None), P("dp", "ctx", None), P("ctx", None))
    return jax.shard_map(
        functools.partial(per_device, mesh.shape["dp"], mesh.shape["ctx"]),
        mesh=mesh,
        in_specs=placed,
        out_specs=(P("dp", "ctx", None), P("ctx", None)),
        check_vma=False,
    )
```

```python
import functools

import jax
import jax.numpy as jnp
from jax import lax
from jax.experimental import pallas as pl
from jax.experimental.pallas import tpu as pltpu
from jax.sharding import PartitionSpec as P

MESH = pl.DeviceIdType.MESH
F32 = jnp.float32
BF16 = jnp.bfloat16
NN = (((1,), (0,)), ((), ()))
NT = (((1,), (1,)), ((), ()))
QUAD = 4


def mm(a, b, dims=NN):
    return lax.dot_general(a, b, dims, preferred_element_type=F32)


def flip(a):
    return jnp.transpose(a.astype(F32)).astype(a.dtype)


def one_minus_exp(y):
    z = y * 0.125
    f = z * (1.0 + z * (1 / 2) * (1.0 + z * (1 / 3) * (1.0 + z * (1 / 4) * (1.0 + z * (1 / 5) * (1.0 + z * (1 / 6) * (1.0 + z * (1 / 7)))))))
    for _ in range(3):
        f = f * (f + 2.0)
    return -f


def partner(place, j):
    out, bit = place, 1
    while bit <= j:
        if j & bit:
            out = out + bit - 2 * bit * lax.rem(place // bit, 2)
        bit *= 2
    return out


def body(line, total_rows, head_count, x_hbm, lr_hbm, g_hbm, w_hbm, gf_ref, gw_ref,
         x_ref, lr_ref, g_ref, w_ref, w_other, xr, xs, xw, gs, xw_far, gs_far, bt, gx, bc_all,
         pm, acc, z_send, z_recv, full,
         in_sem, w_sem, e_sem_s, e_sem_r, x_sem_s, x_sem_r, o_sem, b_sem_s, b_sem_r,
         z_sem_s, z_sem_r, agz_sem_s, agz_sem_r, ag_sem_s, ag_sem_r, m_sem_s, m_sem_r):
    rows, width = x_ref.shape
    shard = w_ref.shape[0]
    state = w_ref.shape[1] // 2
    inv_root = state ** (-0.5)
    dp = lax.axis_index("dp")
    ctx = lax.axis_index("ctx")
    place = lax.rem(dp, QUAD)
    spot = dp // QUAD
    blocks = acc.shape[0]
    per_shard = blocks // 2
    mate = {"ctx": 1 - ctx}
    far_first = (3, 2, 1)
    hubs = [{"dp": spot * QUAD + partner(place, j), "ctx": 1} for j in range(1, QUAD)]
    leaves = [{"dp": spot * QUAD + partner(place, j), "ctx": 0} for j in range(1, QUAD)]
    if line == blocks:
        lines = [{"dp": partner(spot, j) * QUAD + place} for j in range(1, line)]
    else:
        lines = []
        m = 1
        while m < line:
            lines.append({"dp": dp + QUAD * m * (1 - 2 * lax.rem(spot // m, 2))})
            m *= 2

    def remote(src, dst, s_sem, r_sem, who):
        return pltpu.make_async_remote_copy(
            src_ref=src, dst_ref=dst, send_sem=s_sem, recv_sem=r_sem, device_id=who, device_id_type=MESH)

    def send(src, dst, s_sem, r_sem, who):
        copy = remote(src, dst, s_sem, r_sem, who)
        copy.start()
        return copy

    barrier = pltpu.get_barrier_semaphore()

    @pl.when(ctx == 1)
    def _():
        for who in hubs + leaves + lines:
            pl.semaphore_signal(barrier, inc=1, device_id=who, device_id_type=MESH)

    pl.semaphore_signal(barrier, inc=1, device_id=mate, device_id_type=MESH)

    loads = [pltpu.make_async_copy(a, b, in_sem.at[k])
             for k, (a, b) in enumerate(((x_hbm, x_ref), (lr_hbm, lr_ref), (w_hbm, w_ref), (g_hbm, g_ref)))]
    for load in loads:
        load.start()

    own = pl.ds(pl.multiple_of(ctx * shard, shard), shard)
    far = pl.ds(pl.multiple_of((1 - ctx) * shard, shard), shard)

    quarter = shard // QUAD

    def columns(c, q):
        return pl.ds(pl.multiple_of(c * shard + q * quarter, quarter), quarter)

    def band(k):
        return pl.ds(pl.multiple_of(k * rows, rows), rows)

    pl.semaphore_wait(barrier, QUAD + ctx * len(lines))
    w_copy = send(w_hbm, w_other, w_sem.at[0], w_sem.at[1], mate)

    def x_copy(j, c, source, who):
        return remote(x_ref.at[:, columns(c, partner(place, j))], xr.at[j, c, band(source)],
                      x_sem_s.at[j, c], x_sem_r.at[j, source, c], who)

    loads[0].wait()
    x_copies = [x_copy(j, c, ctx, hubs[j - 1]) for j, c in ((3, 0), (3, 1), (1, 0), (2, 0), (1, 1), (2, 1))]
    for copy in x_copies:
        copy.start()
    own_copies = [pltpu.make_async_copy(x_ref.at[:, columns(c, place)], xr.at[0, c, band(ctx)], o_sem.at[c])
                  for c in range(2)]
    mate_copies = [x_copy(0, c, 0, mate) for c in range(2)]

    @pl.when(ctx == 1)
    def _():
        for copy in own_copies:
            copy.start()

    @pl.when(ctx == 0)
    def _():
        for copy in mate_copies:
            copy.start()

    ti = lax.broadcasted_iota(jnp.int32, (rows, rows), 0)
    si = lax.broadcasted_iota(jnp.int32, (rows, rows), 1)
    tri = jnp.where(ti <= si, 1.0, 0.0).astype(F32)
    hi_ = lax.broadcasted_iota(jnp.int32, (rows, width), 0)
    ci_ = lax.broadcasted_iota(jnp.int32, (rows, width), 1)
    head_dim = width // head_count
    lo_c = hi_ * head_dim
    spread = jnp.where((ci_ >= lo_c) & (ci_ < lo_c + head_dim), 1.0, 0.0).astype(BF16)

    loads[1].wait()
    lr = lr_ref[...]
    lr_t = jnp.concatenate([lr, jnp.zeros((rows - head_count, rows), F32)], axis=0)
    incl_t = lax.dot_general(lr_t, tri, NN, precision=lax.Precision.HIGHEST, preferred_element_type=F32)
    excl_t = incl_t - lr_t
    lr_pad = jnp.transpose(lr_t)
    incl = jnp.transpose(incl_t)
    excl = incl - lr_pad
    total = incl[rows - 1:rows, :]
    step = jnp.sqrt(one_minus_exp(2.0 * lr_pad))
    first = ctx == 0
    rate_x = jnp.exp(jnp.where(first, total - incl, excl))
    rate_g = jnp.exp(jnp.where(first, total - excl, incl)) * inv_root

    def widen(v):
        top = v.astype(BF16)
        low = (v - top.astype(F32)).astype(BF16)
        return mm(top, spread) + mm(low, spread)

    step_w = widen(step)
    gx[...] = step_w
    wide_x = widen(rate_x * step)
    loads[2].wait()
    xf = x_ref[...].astype(F32)
    xw[...] = (xf * wide_x).astype(BF16)
    e_copies = [send(xw, xw_far, e_sem_s.at[0], e_sem_r.at[0], mate)]
    loads[3].wait()
    gs[...] = (g_ref[...].astype(F32) * widen(rate_g)).astype(BF16)
    e_copies.append(send(gs, gs_far, e_sem_s.at[1], e_sem_r.at[1], mate))

    bc = mm(x_ref[:, own], w_ref[...])
    w_copy.wait()
    bc = (bc + mm(x_ref[:, far], w_other[...])).astype(BF16)
    b_in = bc[:, :state]
    c_out = bc[:, state:]

    bt[:, :rows] = jnp.concatenate([flip(b_in), flip(c_out)], axis=0)
    e_copies.append(send(bt.at[:, slice(0, rows)], bt.at[:, slice(rows, 2 * rows)],
                         e_sem_s.at[2], e_sem_r.at[2], mate))
    xs[...] = (x_ref[...].astype(F32) * gx[...]).astype(BF16)

    twice = jnp.where(ti == si, 2.0, 1.0).astype(F32)
    dots = mm(b_in, c_out, NT) * (twice * inv_root)
    upper = si >= ti
    lane = lax.broadcasted_iota(jnp.int32, (rows, 2 * head_dim), 1)

    def apart(cols):
        gp = g_ref[:, cols]
        zero = jnp.zeros_like(gp)
        return jnp.concatenate([jnp.where(lane < head_dim, gp, zero), jnp.where(lane < head_dim, zero, gp)], axis=0)

    wb = jnp.zeros((rows, rows), F32)
    for pair in range(head_count // 2):
        cols = slice(pair * 2 * head_dim, (pair + 1) * 2 * head_dim)
        cross = mm(xs[:, cols], apart(cols), NT)
        for j in range(2):
            h = 2 * pair + j
            gap = jnp.where(upper, incl_t[h:h + 1, :] - incl[:, h:h + 1], excl[:, h:h + 1] - excl_t[h:h + 1, :])
            mix = jnp.exp(gap)
            wb = wb + mix * cross[:, j * rows:(j + 1) * rows]
            pm[pair, :, j * rows:(j + 1) * rows] = (mix * dots).astype(BF16)
    wb = (wb * (twice * inv_root)).astype(BF16)
    e_copies[0].wait_recv()
    far_c = mm(xw_far[...], gs[...], NT).astype(BF16)
    e_copies[1].wait_recv()
    far_b = mm(xw[...], gs_far[...], NT).astype(BF16)
    e_copies[2].wait_recv()
    grad_b = mm(bt[state:, :], jnp.concatenate([wb, far_b], axis=1), NT)
    grad_c = mm(bt[:state, :], jnp.concatenate([wb, far_c], axis=0))
    grad_bc = jnp.concatenate([grad_b, grad_c], axis=0).astype(BF16)
    bc_all[0, :, band(ctx)] = grad_bc

    def b_copy(j, source, who):
        return remote(bc_all.at[0, :, band(source)], bc_all.at[j, :, band(source)],
                      b_sem_s.at[j], b_sem_r.at[j, source], who)

    b_copies = [b_copy(j, ctx, hubs[j - 1]) for j in far_first]
    for copy in b_copies:
        copy.start()
    mate_copies.append(b_copy(0, 0, mate))

    @pl.when(ctx == 0)
    def _():
        mate_copies[2].start()

    def finish_features():
        for pair in range(head_count // 2):
            cols = slice(pair * 2 * head_dim, (pair + 1) * 2 * head_dim)
            gx[:, cols] = gx[:, cols] * mm(pm[pair], apart(cols))
        gx[...] = mm(mm(b_in, bt[state:, rows:]).astype(BF16), gs_far[...]) * wide_x + gx[...]
        left = flip(grad_bc)
        gf_ref[:, own] = (gx[:, own] + mm(left, w_ref[...], NT)).astype(BF16)
        gf_ref[:, far] = (gx[:, far] + mm(left, w_other[...], NT)).astype(BF16)

    finish_features()

    scale = total_rows ** (-0.5)
    parts = 2
    h = 2 * state // parts
    parts_of = [slice(p * h, (p + 1) * h) for p in range(parts)]
    size = acc.shape[2]

    def gather_copy(j, t, p, k):
        return remote(full.at[j, :, parts_of[p]], gw_ref.at[place, lax.rem(t, per_shard), :, parts_of[p]],
                      ag_sem_s.at[j, k - 1, p], ag_sem_r.at[k - 1, lax.rem(t, per_shard), p],
                      {"dp": spot * QUAD + partner(place, k), "ctx": t // per_shard})

    def mate_copy(j, t, p):
        return remote(full.at[j, :, parts_of[p]], gw_ref.at[place, lax.rem(t, per_shard), :, parts_of[p]],
                      m_sem_s.at[j, p], m_sem_r.at[lax.rem(t, per_shard), p], mate)

    def spread_out(me, j, t, p):
        for k in far_first:
            gather_copy(j, t, p, k).start()

        @pl.when(t // per_shard != me)
        def _():
            mate_copy(j, t, p).start()

        @pl.when(t // per_shard == me)
        def _():
            gw_ref[place, lax.rem(t, per_shard), :, parts_of[p]] = full[j, :, parts_of[p]]

    def settle(me, j, t, p):
        for k in far_first:
            gather_copy(j, t, p, k).wait_send()

        @pl.when(t // per_shard != me)
        def _():
            mate_copy(j, t, p).wait_send()

    if line == blocks:
        owner = [partner(spot, j) for j in range(line)]
        handler = (1, 0, 1, 1)
    else:
        owner = [jnp.int32(t) for t in range(blocks)]
        handler = (1,) * blocks

    def along(j, p):
        return remote(full.at[0, :, parts_of[p]], full.at[j, :, parts_of[p]],
                      agz_sem_s.at[j - 1, p], agz_sem_r.at[j - 1, p], {**lines[j - 1], "ctx": handler[j]})

    def turned(v):
        return jnp.transpose(v * scale).astype(BF16)

    @pl.when(ctx == 1)
    def _():
        for copy in own_copies:
            copy.wait()
        for c in range(2):
            mate_copies[c].wait_recv()
        mate_copies[2].wait_recv()
        for j in far_first:
            for source in range(2):
                for c in range(2):
                    x_copy(j, c, source, hubs[j - 1]).wait_recv()
        total_t = [mm(bc_all[0], xr[0, c]) for c in range(2)]
        for j in far_first:
            for source in range(2):
                b_copy(j, source, hubs[j - 1]).wait_recv()
            total_t = [total_t[c] + mm(bc_all[j], xr[j, c]) for c in range(2)]
        for t in range(blocks):
            i = t % per_shard
            acc[t] = total_t[t // per_shard][:, i * size:(i + 1) * size]

        if line == blocks:
            order = range(1, line)

            def z_copy(j, p):
                return remote(z_send.at[j - 1, 0, parts_of[p]], z_recv.at[j - 1, 0, parts_of[p]],
                              z_sem_s.at[j - 1, p], z_sem_r.at[j - 1, p], lines[j - 1])

            for p in range(parts):
                for j in reversed(order):
                    z_send[j - 1, 0, parts_of[p]] = acc[owner[j], parts_of[p]].astype(BF16)
                    z_copy(j, p).start()
            for p in range(parts):
                whole = acc[spot, parts_of[p]]
                for j in order:
                    z_copy(j, p).wait_recv()
                    whole = whole + z_recv[j - 1, 0, parts_of[p]].astype(F32)
                full[0, :, parts_of[p]] = turned(whole)
                for j in order:
                    along(j, p).start()
                spread_out(1, 0, spot, p)
            for p in range(parts):
                for j in order:
                    if handler[j] == 1:
                        along(j, p).wait_recv()
                        spread_out(1, j, owner[j], p)
            for p in range(parts):
                for j in order:
                    z_copy(j, p).wait_send()
                    along(j, p).wait_send()
        else:
            for k in range(len(lines)):
                z_send[k] = acc[...].astype(BF16)
                copy = send(z_send.at[k], z_recv.at[k], z_sem_s.at[k, 0], z_sem_r.at[k, 0], lines[k])
                copy.wait()
                acc[...] = z_send[k].astype(F32) + z_recv[k].astype(F32)
            for t in range(blocks):
                for p in range(parts):
                    full[t, :, parts_of[p]] = turned(acc[t, parts_of[p]])
                    spread_out(1, t, owner[t], p)
        for j in range(blocks):
            for p in range(parts):
                if handler[j] == 1:
                    settle(1, j, owner[j], p)
                else:
                    @pl.when(owner[j] // per_shard == 1)
                    def _():
                        mate_copy(j, owner[j], p).wait_recv()

    @pl.when(ctx == 0)
    def _():
        for p in range(parts):
            for j in range(blocks):
                if handler[j] == 0:
                    along(j, p).wait_recv()
                    spread_out(0, j, owner[j], p)
        for j in range(blocks):
            for p in range(parts):
                if handler[j] == 0:
                    settle(0, j, owner[j], p)
                else:
                    @pl.when(owner[j] // per_shard == 0)
                    def _():
                        mate_copy(j, owner[j], p).wait_recv()

    for k in far_first:
        for i in range(per_shard):
            for p in range(parts):
                gather_copy(0, i, p, k).wait_recv()
    for copy in x_copies + b_copies + e_copies:
        copy.wait_send()

    @pl.when(ctx == 0)
    def _():
        for copy in mate_copies:
            copy.wait_send()


def deliver(gf_ref, gw_ref, gf_hbm, gw_hbm, sem):
    copies = [pltpu.make_async_copy(a, b, sem.at[k]) for k, (a, b) in enumerate(((gf_ref, gf_hbm), (gw_ref, gw_hbm)))]
    for copy in copies:
        copy.start()
    for copy in copies:
        copy.wait()


def per_device(dp_count, ctx_count, features, log_decays, cotangent, bc_weight):
    x, lr, g = features[0], jnp.swapaxes(log_decays[0], 0, 1), cotangent[0]
    rows, width = x.shape
    shard, cols = bc_weight.shape
    total_rows = features.shape[0] * dp_count * rows * ctx_count
    head_count = lr.shape[0]
    line = dp_count // QUAD
    quarter = shard // QUAD
    size = 128
    blocks = 2 * quarter // size
    direct = line == blocks
    hops = max(line - 1 if direct else line.bit_length() - 1, 1)
    deep = 1 if direct else blocks
    dma = pltpu.SemaphoreType.DMA
    vm = pl.BlockSpec(memory_space=pltpu.VMEM)
    gf, gw = pl.pallas_call(
        functools.partial(body, line, total_rows, head_count),
        out_shape=(pltpu.VMEM((rows, width), BF16), pltpu.VMEM((QUAD, blocks // 2, size, cols), BF16)),
        in_specs=[pl.BlockSpec(memory_space=pltpu.HBM)] * 4,
        out_specs=(vm, vm),
        scratch_shapes=[
            pltpu.VMEM((rows, width), BF16),
            pltpu.VMEM((head_count, rows), F32),
            pltpu.VMEM((rows, width), BF16),
            pltpu.VMEM((shard, cols), BF16),
            pltpu.VMEM((shard, cols), BF16),
            pltpu.VMEM((QUAD, 2, 2 * rows, quarter), BF16),
            pltpu.VMEM((rows, width), BF16),
            pltpu.VMEM((rows, width), BF16),
            pltpu.VMEM((rows, width), BF16),
            pltpu.VMEM((rows, width), BF16),
            pltpu.VMEM((rows, width), BF16),
            pltpu.VMEM((cols, 2 * rows), BF16),
            pltpu.VMEM((rows, width), F32),
            pltpu.VMEM((QUAD, cols, 2 * rows), BF16),
            pltpu.VMEM((head_count // 2, rows, 2 * rows), BF16),
            pltpu.VMEM((blocks, cols, size), F32),
            pltpu.VMEM((hops, deep, cols, size), BF16),
            pltpu.VMEM((hops, deep, cols, size), BF16),
            pltpu.VMEM((blocks, size, cols), BF16),
            dma((4,)), dma((2,)), dma((3,)), dma((3,)),
            dma((QUAD, 2)), dma((QUAD, 2, 2)), dma((2,)), dma((QUAD,)), dma((QUAD, 2)),
            dma((hops, 2)), dma((hops, 2)), dma((hops, 2)), dma((hops, 2)),
            dma((blocks, QUAD - 1, 2)), dma((QUAD - 1, blocks // 2, 2)), dma((blocks, 2)), dma((blocks // 2, 2)),
        ],
        compiler_params=pltpu.CompilerParams(
            collective_id=0, has_side_effects=True, vmem_limit_bytes=64256 * 1024),
    )(x, lr, g, bc_weight)
    gw = gw.reshape(shard, cols)
    hbm = pl.BlockSpec(memory_space=pltpu.HBM)
    gf, gw = pl.pallas_call(
        deliver,
        out_shape=(jax.ShapeDtypeStruct((rows, width), BF16), jax.ShapeDtypeStruct((shard, cols), BF16)),
        in_specs=[vm, vm],
        out_specs=(hbm, hbm),
        scratch_shapes=[dma((2,))],
        compiler_params=pltpu.CompilerParams(vmem_limit_bytes=2 * 2**20),
    )(gf, gw)
    return gf[None], gw


def solution(mesh):
    placed = (P("dp", "ctx", None), P("dp", "ctx", None), P("dp", "ctx", None), P("ctx", None))
    return jax.shard_map(
        functools.partial(per_device, mesh.shape["dp"], mesh.shape["ctx"]),
        mesh=mesh,
        in_specs=placed,
        out_specs=(P("dp", "ctx", None), P("ctx", None)),
        check_vma=False,
    )
```

```python
import functools

import jax
import jax.numpy as jnp
from jax import lax
from jax.experimental import pallas as pl
from jax.experimental.pallas import tpu as pltpu
from jax.sharding import PartitionSpec as P

MESH = pl.DeviceIdType.MESH
F32 = jnp.float32
BF16 = jnp.bfloat16
NN = (((1,), (0,)), ((), ()))
NT = (((1,), (1,)), ((), ()))
QUAD = 4


def mm(a, b, dims=NN):
    return lax.dot_general(a, b, dims, preferred_element_type=F32)


def flip(a):
    return jnp.transpose(a.astype(F32)).astype(a.dtype)


def one_minus_exp(y):
    z = y * 0.125
    f = z * (1.0 + z * (1 / 2) * (1.0 + z * (1 / 3) * (1.0 + z * (1 / 4) * (1.0 + z * (1 / 5) * (1.0 + z * (1 / 6) * (1.0 + z * (1 / 7)))))))
    for _ in range(3):
        f = f * (f + 2.0)
    return -f


def partner(place, j):
    out, bit = place, 1
    while bit <= j:
        if j & bit:
            out = out + bit - 2 * bit * lax.rem(place // bit, 2)
        bit *= 2
    return out


def body(line, total_rows, head_count, x_hbm, lr_hbm, g_hbm, w_hbm, gf_ref, gw_ref,
         x_ref, lr_ref, g_ref, w_ref, w_other, xr, xs, xw, gs, xw_far, gs_far, bt, gx, bc_all,
         pm, acc, z_send, z_recv, full,
         in_sem, w_sem, e_sem_s, e_sem_r, x_sem_s, x_sem_r, o_sem, b_sem_s, b_sem_r,
         z_sem_s, z_sem_r, agz_sem_s, agz_sem_r, ag_sem_s, ag_sem_r, m_sem_s, m_sem_r):
    rows, width = x_ref.shape
    shard = w_ref.shape[0]
    state = w_ref.shape[1] // 2
    inv_root = state ** (-0.5)
    dp = lax.axis_index("dp")
    ctx = lax.axis_index("ctx")
    place = lax.rem(dp, QUAD)
    spot = dp // QUAD
    blocks = acc.shape[0]
    per_shard = blocks // 2
    mate = {"ctx": 1 - ctx}
    far_first = (3, 2, 1)
    hubs = [{"dp": spot * QUAD + partner(place, j), "ctx": 1} for j in range(1, QUAD)]
    leaves = [{"dp": spot * QUAD + partner(place, j), "ctx": 0} for j in range(1, QUAD)]
    if line == blocks:
        lines = [{"dp": partner(spot, j) * QUAD + place} for j in range(1, line)]
    else:
        lines = []
        m = 1
        while m < line:
            lines.append({"dp": dp + QUAD * m * (1 - 2 * lax.rem(spot // m, 2))})
            m *= 2

    def remote(src, dst, s_sem, r_sem, who):
        return pltpu.make_async_remote_copy(
            src_ref=src, dst_ref=dst, send_sem=s_sem, recv_sem=r_sem, device_id=who, device_id_type=MESH)

    def send(src, dst, s_sem, r_sem, who):
        copy = remote(src, dst, s_sem, r_sem, who)
        copy.start()
        return copy

    barrier = pltpu.get_barrier_semaphore()

    @pl.when(ctx == 1)
    def _():
        for who in hubs + leaves + lines:
            pl.semaphore_signal(barrier, inc=1, device_id=who, device_id_type=MESH)

    pl.semaphore_signal(barrier, inc=1, device_id=mate, device_id_type=MESH)

    loads = [pltpu.make_async_copy(a, b, in_sem.at[k])
             for k, (a, b) in enumerate(((x_hbm, x_ref), (lr_hbm, lr_ref), (w_hbm, w_ref), (g_hbm, g_ref)))]
    for load in loads:
        load.start()

    own = pl.ds(pl.multiple_of(ctx * shard, shard), shard)
    far = pl.ds(pl.multiple_of((1 - ctx) * shard, shard), shard)

    quarter = shard // QUAD

    def columns(c, q):
        return pl.ds(pl.multiple_of(c * shard + q * quarter, quarter), quarter)

    def band(k):
        return pl.ds(pl.multiple_of(k * rows, rows), rows)

    pl.semaphore_wait(barrier, QUAD + ctx * len(lines))
    w_copy = send(w_hbm, w_other, w_sem.at[0], w_sem.at[1], mate)

    def x_copy(j, c, source, who):
        return remote(x_ref.at[:, columns(c, partner(place, j))], xr.at[j, c, band(source)],
                      x_sem_s.at[j, c], x_sem_r.at[j, source, c], who)

    loads[0].wait()
    x_copies = [x_copy(j, c, ctx, hubs[j - 1]) for j, c in ((3, 0), (3, 1), (1, 0), (2, 0), (1, 1), (2, 1))]
    for copy in x_copies:
        copy.start()
    own_copies = [pltpu.make_async_copy(x_ref.at[:, columns(c, place)], xr.at[0, c, band(ctx)], o_sem.at[c])
                  for c in range(2)]
    mate_copies = [x_copy(0, c, 0, mate) for c in range(2)]

    @pl.when(ctx == 1)
    def _():
        for copy in own_copies:
            copy.start()

    @pl.when(ctx == 0)
    def _():
        for copy in mate_copies:
            copy.start()

    ti = lax.broadcasted_iota(jnp.int32, (rows, rows), 0)
    si = lax.broadcasted_iota(jnp.int32, (rows, rows), 1)
    tri = jnp.where(ti <= si, 1.0, 0.0).astype(F32)
    hi_ = lax.broadcasted_iota(jnp.int32, (rows, width), 0)
    ci_ = lax.broadcasted_iota(jnp.int32, (rows, width), 1)
    head_dim = width // head_count
    lo_c = hi_ * head_dim
    spread = jnp.where((ci_ >= lo_c) & (ci_ < lo_c + head_dim), 1.0, 0.0).astype(BF16)

    loads[1].wait()
    lr = lr_ref[...]
    lr_t = jnp.concatenate([lr, jnp.zeros((rows - head_count, rows), F32)], axis=0)
    incl_t = lax.dot_general(lr_t, tri, NN, precision=lax.Precision.HIGHEST, preferred_element_type=F32)
    excl_t = incl_t - lr_t
    lr_pad = jnp.transpose(lr_t)
    incl = jnp.transpose(incl_t)
    excl = incl - lr_pad
    total = incl[rows - 1:rows, :]
    step = jnp.sqrt(one_minus_exp(2.0 * lr_pad))
    first = ctx == 0
    rate_x = jnp.exp(jnp.where(first, total - incl, excl))
    rate_g = jnp.exp(jnp.where(first, total - excl, incl)) * inv_root

    twofold = jnp.concatenate([spread, spread], axis=0)

    def widen(v):
        top = v.astype(BF16)
        low = (v - top.astype(F32)).astype(BF16)
        return mm(jnp.concatenate([top, low], axis=1), twofold)

    wide = widen(jnp.concatenate([step, rate_x * step, rate_g], axis=0))
    step_w, wide_x, wide_g = (wide[k * rows:(k + 1) * rows] for k in range(3))
    gx[...] = step_w
    loads[2].wait()
    xf = x_ref[...].astype(F32)
    xw[...] = (xf * wide_x).astype(BF16)
    e_copies = [send(xw, xw_far, e_sem_s.at[0], e_sem_r.at[0], mate)]
    loads[3].wait()
    gs[...] = (g_ref[...].astype(F32) * wide_g).astype(BF16)
    e_copies.append(send(gs, gs_far, e_sem_s.at[1], e_sem_r.at[1], mate))

    bc = mm(x_ref[:, own], w_ref[...])
    w_copy.wait()
    bc = (bc + mm(x_ref[:, far], w_other[...])).astype(BF16)
    b_in = bc[:, :state]
    c_out = bc[:, state:]

    bt[:, :rows] = jnp.concatenate([flip(b_in), flip(c_out)], axis=0)
    e_copies.append(send(bt.at[:, slice(0, rows)], bt.at[:, slice(rows, 2 * rows)],
                         e_sem_s.at[2], e_sem_r.at[2], mate))
    xs[...] = (x_ref[...].astype(F32) * gx[...]).astype(BF16)

    twice = jnp.where(ti == si, 2.0, 1.0).astype(F32)
    dots = mm(b_in, c_out, NT) * (twice * inv_root)
    upper = si >= ti
    lane = lax.broadcasted_iota(jnp.int32, (rows, 2 * head_dim), 1)

    def apart(cols):
        gp = g_ref[:, cols]
        zero = jnp.zeros_like(gp)
        return jnp.concatenate([jnp.where(lane < head_dim, gp, zero), jnp.where(lane < head_dim, zero, gp)], axis=0)

    wb = jnp.zeros((rows, rows), F32)
    for pair in range(head_count // 2):
        cols = slice(pair * 2 * head_dim, (pair + 1) * 2 * head_dim)
        cross = mm(xs[:, cols], apart(cols), NT)
        for j in range(2):
            h = 2 * pair + j
            gap = jnp.where(upper, incl_t[h:h + 1, :] - incl[:, h:h + 1], excl[:, h:h + 1] - excl_t[h:h + 1, :])
            mix = jnp.exp(gap)
            wb = wb + mix * cross[:, j * rows:(j + 1) * rows]
            pm[pair, :, j * rows:(j + 1) * rows] = (mix * dots).astype(BF16)
    wb = (wb * (twice * inv_root)).astype(BF16)
    e_copies[0].wait_recv()
    far_c = mm(xw_far[...], gs[...], NT).astype(BF16)
    e_copies[1].wait_recv()
    far_b = mm(xw[...], gs_far[...], NT).astype(BF16)
    e_copies[2].wait_recv()
    grad_b = mm(bt[state:, :], jnp.concatenate([wb, far_b], axis=1), NT)
    grad_c = mm(bt[:state, :], jnp.concatenate([wb, far_c], axis=0))
    grad_bc = jnp.concatenate([grad_b, grad_c], axis=0).astype(BF16)
    bc_all[0, :, band(ctx)] = grad_bc

    def b_copy(j, source, who):
        return remote(bc_all.at[0, :, band(source)], bc_all.at[j, :, band(source)],
                      b_sem_s.at[j], b_sem_r.at[j, source], who)

    b_copies = [b_copy(j, ctx, hubs[j - 1]) for j in far_first]
    for copy in b_copies:
        copy.start()
    mate_copies.append(b_copy(0, 0, mate))

    @pl.when(ctx == 0)
    def _():
        mate_copies[2].start()

    def finish_features():
        for pair in range(head_count // 2):
            cols = slice(pair * 2 * head_dim, (pair + 1) * 2 * head_dim)
            gx[:, cols] = gx[:, cols] * mm(pm[pair], apart(cols))
        gx[...] = mm(mm(b_in, bt[state:, rows:]).astype(BF16), gs_far[...]) * wide_x + gx[...]
        left = flip(grad_bc)
        gf_ref[:, own] = (gx[:, own] + mm(left, w_ref[...], NT)).astype(BF16)
        gf_ref[:, far] = (gx[:, far] + mm(left, w_other[...], NT)).astype(BF16)

    finish_features()

    scale = total_rows ** (-0.5)
    parts = 2
    h = 2 * state // parts
    parts_of = [slice(p * h, (p + 1) * h) for p in range(parts)]
    size = acc.shape[2]

    def gather_copy(j, t, p, k):
        return remote(full.at[j, :, parts_of[p]], gw_ref.at[place, lax.rem(t, per_shard), :, parts_of[p]],
                      ag_sem_s.at[j, k - 1, p], ag_sem_r.at[k - 1, lax.rem(t, per_shard), p],
                      {"dp": spot * QUAD + partner(place, k), "ctx": t // per_shard})

    def mate_copy(j, t, p):
        return remote(full.at[j, :, parts_of[p]], gw_ref.at[place, lax.rem(t, per_shard), :, parts_of[p]],
                      m_sem_s.at[j, p], m_sem_r.at[lax.rem(t, per_shard), p], mate)

    def spread_out(me, j, t, p):
        for k in far_first:
            gather_copy(j, t, p, k).start()

        @pl.when(t // per_shard != me)
        def _():
            mate_copy(j, t, p).start()

        @pl.when(t // per_shard == me)
        def _():
            gw_ref[place, lax.rem(t, per_shard), :, parts_of[p]] = full[j, :, parts_of[p]]

    def settle(me, j, t, p):
        for k in far_first:
            gather_copy(j, t, p, k).wait_send()

        @pl.when(t // per_shard != me)
        def _():
            mate_copy(j, t, p).wait_send()

    if line == blocks:
        owner = [partner(spot, j) for j in range(line)]
        handler = (1, 0, 1, 1)
    else:
        owner = [jnp.int32(t) for t in range(blocks)]
        handler = (1,) * blocks

    def along(j, p):
        return remote(full.at[0, :, parts_of[p]], full.at[j, :, parts_of[p]],
                      agz_sem_s.at[j - 1, p], agz_sem_r.at[j - 1, p], {**lines[j - 1], "ctx": handler[j]})

    def turned(v):
        return jnp.transpose(v * scale).astype(BF16)

    @pl.when(ctx == 1)
    def _():
        for copy in own_copies:
            copy.wait()
        for c in range(2):
            mate_copies[c].wait_recv()
        mate_copies[2].wait_recv()
        for j in far_first:
            for source in range(2):
                for c in range(2):
                    x_copy(j, c, source, hubs[j - 1]).wait_recv()
        total_t = [mm(bc_all[0], xr[0, c]) for c in range(2)]
        for j in far_first:
            for source in range(2):
                b_copy(j, source, hubs[j - 1]).wait_recv()
            total_t = [total_t[c] + mm(bc_all[j], xr[j, c]) for c in range(2)]
        for t in range(blocks):
            i = t % per_shard
            acc[t] = total_t[t // per_shard][:, i * size:(i + 1) * size]

        if line == blocks:
            order = range(1, line)

            def z_copy(j, p):
                return remote(z_send.at[j - 1, 0, parts_of[p]], z_recv.at[j - 1, 0, parts_of[p]],
                              z_sem_s.at[j - 1, p], z_sem_r.at[j - 1, p], lines[j - 1])

            for p in range(parts):
                for j in reversed(order):
                    z_send[j - 1, 0, parts_of[p]] = acc[owner[j], parts_of[p]].astype(BF16)
                    z_copy(j, p).start()
            for p in range(parts):
                whole = acc[spot, parts_of[p]]
                for j in order:
                    z_copy(j, p).wait_recv()
                    whole = whole + z_recv[j - 1, 0, parts_of[p]].astype(F32)
                full[0, :, parts_of[p]] = turned(whole)
                for j in order:
                    along(j, p).start()
                spread_out(1, 0, spot, p)
            for p in range(parts):
                for j in order:
                    if handler[j] == 1:
                        along(j, p).wait_recv()
                        spread_out(1, j, owner[j], p)
            for p in range(parts):
                for j in order:
                    z_copy(j, p).wait_send()
                    along(j, p).wait_send()
        else:
            for k in range(len(lines)):
                z_send[k] = acc[...].astype(BF16)
                copy = send(z_send.at[k], z_recv.at[k], z_sem_s.at[k, 0], z_sem_r.at[k, 0], lines[k])
                copy.wait()
                acc[...] = z_send[k].astype(F32) + z_recv[k].astype(F32)
            for t in range(blocks):
                for p in range(parts):
                    full[t, :, parts_of[p]] = turned(acc[t, parts_of[p]])
                    spread_out(1, t, owner[t], p)
        for j in range(blocks):
            for p in range(parts):
                if handler[j] == 1:
                    settle(1, j, owner[j], p)
                else:
                    @pl.when(owner[j] // per_shard == 1)
                    def _():
                        mate_copy(j, owner[j], p).wait_recv()

    @pl.when(ctx == 0)
    def _():
        for p in range(parts):
            for j in range(blocks):
                if handler[j] == 0:
                    along(j, p).wait_recv()
                    spread_out(0, j, owner[j], p)
        for j in range(blocks):
            for p in range(parts):
                if handler[j] == 0:
                    settle(0, j, owner[j], p)
                else:
                    @pl.when(owner[j] // per_shard == 0)
                    def _():
                        mate_copy(j, owner[j], p).wait_recv()

    for k in far_first:
        for i in range(per_shard):
            for p in range(parts):
                gather_copy(0, i, p, k).wait_recv()
    for copy in x_copies + b_copies + e_copies:
        copy.wait_send()

    @pl.when(ctx == 0)
    def _():
        for copy in mate_copies:
            copy.wait_send()


def deliver(gf_ref, gw_ref, gf_hbm, gw_hbm, sem):
    copies = [pltpu.make_async_copy(a, b, sem.at[k]) for k, (a, b) in enumerate(((gf_ref, gf_hbm), (gw_ref, gw_hbm)))]
    for copy in copies:
        copy.start()
    for copy in copies:
        copy.wait()


def per_device(dp_count, ctx_count, features, log_decays, cotangent, bc_weight):
    x, lr, g = features[0], jnp.swapaxes(log_decays[0], 0, 1), cotangent[0]
    rows, width = x.shape
    shard, cols = bc_weight.shape
    total_rows = features.shape[0] * dp_count * rows * ctx_count
    head_count = lr.shape[0]
    line = dp_count // QUAD
    quarter = shard // QUAD
    size = 128
    blocks = 2 * quarter // size
    direct = line == blocks
    hops = max(line - 1 if direct else line.bit_length() - 1, 1)
    deep = 1 if direct else blocks
    dma = pltpu.SemaphoreType.DMA
    vm = pl.BlockSpec(memory_space=pltpu.VMEM)
    gf, gw = pl.pallas_call(
        functools.partial(body, line, total_rows, head_count),
        out_shape=(pltpu.VMEM((rows, width), BF16), pltpu.VMEM((QUAD, blocks // 2, size, cols), BF16)),
        in_specs=[pl.BlockSpec(memory_space=pltpu.HBM)] * 4,
        out_specs=(vm, vm),
        scratch_shapes=[
            pltpu.VMEM((rows, width), BF16),
            pltpu.VMEM((head_count, rows), F32),
            pltpu.VMEM((rows, width), BF16),
            pltpu.VMEM((shard, cols), BF16),
            pltpu.VMEM((shard, cols), BF16),
            pltpu.VMEM((QUAD, 2, 2 * rows, quarter), BF16),
            pltpu.VMEM((rows, width), BF16),
            pltpu.VMEM((rows, width), BF16),
            pltpu.VMEM((rows, width), BF16),
            pltpu.VMEM((rows, width), BF16),
            pltpu.VMEM((rows, width), BF16),
            pltpu.VMEM((cols, 2 * rows), BF16),
            pltpu.VMEM((rows, width), F32),
            pltpu.VMEM((QUAD, cols, 2 * rows), BF16),
            pltpu.VMEM((head_count // 2, rows, 2 * rows), BF16),
            pltpu.VMEM((blocks, cols, size), F32),
            pltpu.VMEM((hops, deep, cols, size), BF16),
            pltpu.VMEM((hops, deep, cols, size), BF16),
            pltpu.VMEM((blocks, size, cols), BF16),
            dma((4,)), dma((2,)), dma((3,)), dma((3,)),
            dma((QUAD, 2)), dma((QUAD, 2, 2)), dma((2,)), dma((QUAD,)), dma((QUAD, 2)),
            dma((hops, 2)), dma((hops, 2)), dma((hops, 2)), dma((hops, 2)),
            dma((blocks, QUAD - 1, 2)), dma((QUAD - 1, blocks // 2, 2)), dma((blocks, 2)), dma((blocks // 2, 2)),
        ],
        compiler_params=pltpu.CompilerParams(
            collective_id=0, has_side_effects=True, vmem_limit_bytes=64256 * 1024),
    )(x, lr, g, bc_weight)
    gw = gw.reshape(shard, cols)
    hbm = pl.BlockSpec(memory_space=pltpu.HBM)
    gf, gw = pl.pallas_call(
        deliver,
        out_shape=(jax.ShapeDtypeStruct((rows, width), BF16), jax.ShapeDtypeStruct((shard, cols), BF16)),
        in_specs=[vm, vm],
        out_specs=(hbm, hbm),
        scratch_shapes=[dma((2,))],
        compiler_params=pltpu.CompilerParams(vmem_limit_bytes=2 * 2**20),
    )(gf, gw)
    return gf[None], gw


def solution(mesh):
    placed = (P("dp", "ctx", None), P("dp", "ctx", None), P("dp", "ctx", None), P("ctx", None))
    return jax.shard_map(
        functools.partial(per_device, mesh.shape["dp"], mesh.shape["ctx"]),
        mesh=mesh,
        in_specs=placed,
        out_specs=(P("dp", "ctx", None), P("ctx", None)),
        check_vma=False,
    )
```

```python
import functools

import jax
import jax.numpy as jnp
from jax import lax
from jax.experimental import pallas as pl
from jax.experimental.pallas import tpu as pltpu
from jax.sharding import PartitionSpec as P

MESH = pl.DeviceIdType.MESH
F32 = jnp.float32
BF16 = jnp.bfloat16
NN = (((1,), (0,)), ((), ()))
NT = (((1,), (1,)), ((), ()))
QUAD = 4


def mm(a, b, dims=NN):
    return lax.dot_general(a, b, dims, preferred_element_type=F32)


def flip(a):
    return jnp.transpose(a.astype(F32)).astype(a.dtype)


def one_minus_exp(y):
    z = y * 0.125
    f = z * (1.0 + z * (1 / 2) * (1.0 + z * (1 / 3) * (1.0 + z * (1 / 4) * (1.0 + z * (1 / 5) * (1.0 + z * (1 / 6) * (1.0 + z * (1 / 7)))))))
    for _ in range(3):
        f = f * (f + 2.0)
    return -f


def partner(place, j):
    out, bit = place, 1
    while bit <= j:
        if j & bit:
            out = out + bit - 2 * bit * lax.rem(place // bit, 2)
        bit *= 2
    return out


def body(line, total_rows, head_count, x_hbm, lr_hbm, g_hbm, w_hbm, gf_ref, gw_ref,
         x_ref, lr_ref, g_ref, w_ref, w_other, xr, xs, xw, gs, xw_far, gs_far, bt, gx, bc_all,
         pm, acc, z_send, z_recv, full,
         in_sem, w_sem, e_sem_s, e_sem_r, x_sem_s, x_sem_r, o_sem, b_sem_s, b_sem_r,
         z_sem_s, z_sem_r, agz_sem_s, agz_sem_r, ag_sem_s, ag_sem_r, m_sem_s, m_sem_r):
    rows, width = x_ref.shape
    shard = w_ref.shape[0]
    state = w_ref.shape[1] // 2
    inv_root = state ** (-0.5)
    dp = lax.axis_index("dp")
    ctx = lax.axis_index("ctx")
    place = lax.rem(dp, QUAD)
    spot = dp // QUAD
    blocks = acc.shape[0]
    per_shard = blocks // 2
    mate = {"ctx": 1 - ctx}
    far_first = (3, 2, 1)
    hubs = [{"dp": spot * QUAD + partner(place, j), "ctx": 1} for j in range(1, QUAD)]
    leaves = [{"dp": spot * QUAD + partner(place, j), "ctx": 0} for j in range(1, QUAD)]
    if line == blocks:
        lines = [{"dp": partner(spot, j) * QUAD + place} for j in range(1, line)]
    else:
        lines = []
        m = 1
        while m < line:
            lines.append({"dp": dp + QUAD * m * (1 - 2 * lax.rem(spot // m, 2))})
            m *= 2

    def remote(src, dst, s_sem, r_sem, who):
        return pltpu.make_async_remote_copy(
            src_ref=src, dst_ref=dst, send_sem=s_sem, recv_sem=r_sem, device_id=who, device_id_type=MESH)

    def send(src, dst, s_sem, r_sem, who):
        copy = remote(src, dst, s_sem, r_sem, who)
        copy.start()
        return copy

    barrier = pltpu.get_barrier_semaphore()

    @pl.when(ctx == 1)
    def _():
        for who in hubs + leaves + lines:
            pl.semaphore_signal(barrier, inc=1, device_id=who, device_id_type=MESH)

    pl.semaphore_signal(barrier, inc=1, device_id=mate, device_id_type=MESH)

    loads = [pltpu.make_async_copy(a, b, in_sem.at[k])
             for k, (a, b) in enumerate(((x_hbm, x_ref), (lr_hbm, lr_ref), (w_hbm, w_ref), (g_hbm, g_ref)))]
    for load in loads:
        load.start()

    own = pl.ds(pl.multiple_of(ctx * shard, shard), shard)
    far = pl.ds(pl.multiple_of((1 - ctx) * shard, shard), shard)

    quarter = shard // QUAD

    def columns(c, q):
        return pl.ds(pl.multiple_of(c * shard + q * quarter, quarter), quarter)

    def band(k):
        return pl.ds(pl.multiple_of(k * rows, rows), rows)

    pl.semaphore_wait(barrier, QUAD + ctx * len(lines))
    w_copy = send(w_hbm, w_other, w_sem.at[0], w_sem.at[1], mate)

    def x_copy(j, c, source, who):
        return remote(x_ref.at[:, columns(c, partner(place, j))], xr.at[j, c, band(source)],
                      x_sem_s.at[j, c], x_sem_r.at[j, source, c], who)

    loads[0].wait()
    x_copies = [x_copy(j, c, ctx, hubs[j - 1]) for j, c in ((3, 0), (3, 1), (1, 0), (2, 0), (1, 1), (2, 1))]
    for copy in x_copies:
        copy.start()
    own_copies = [pltpu.make_async_copy(x_ref.at[:, columns(c, place)], xr.at[0, c, band(ctx)], o_sem.at[c])
                  for c in range(2)]
    mate_copies = [x_copy(0, c, 0, mate) for c in range(2)]

    @pl.when(ctx == 1)
    def _():
        for copy in own_copies:
            copy.start()

    @pl.when(ctx == 0)
    def _():
        for copy in mate_copies:
            copy.start()

    ti = lax.broadcasted_iota(jnp.int32, (rows, rows), 0)
    si = lax.broadcasted_iota(jnp.int32, (rows, rows), 1)
    tri = jnp.where(ti <= si, 1.0, 0.0).astype(F32)
    hi_ = lax.broadcasted_iota(jnp.int32, (rows, width), 0)
    ci_ = lax.broadcasted_iota(jnp.int32, (rows, width), 1)
    head_dim = width // head_count
    lo_c = hi_ * head_dim
    spread = jnp.where((ci_ >= lo_c) & (ci_ < lo_c + head_dim), 1.0, 0.0).astype(BF16)

    loads[1].wait()
    lr = lr_ref[...]
    lr_t = jnp.concatenate([lr, jnp.zeros((rows - head_count, rows), F32)], axis=0)
    incl_t = lax.dot_general(lr_t, tri, NN, precision=lax.Precision.HIGHEST, preferred_element_type=F32)
    excl_t = incl_t - lr_t
    lr_pad = jnp.transpose(lr_t)
    incl = jnp.transpose(incl_t)
    excl = incl - lr_pad
    total = incl[rows - 1:rows, :]
    step = jnp.sqrt(one_minus_exp(2.0 * lr_pad))
    first = ctx == 0
    rate_x = jnp.exp(jnp.where(first, total - incl, excl))
    rate_g = jnp.exp(jnp.where(first, total - excl, incl)) * inv_root

    twofold = jnp.concatenate([spread, spread], axis=0)

    def widen(v):
        top = v.astype(BF16)
        low = (v - top.astype(F32)).astype(BF16)
        return mm(jnp.concatenate([top, low], axis=1), twofold)

    wide = widen(jnp.concatenate([step, rate_x * step, rate_g], axis=0))
    step_w, wide_x, wide_g = (wide[k * rows:(k + 1) * rows] for k in range(3))
    gx[...] = step_w
    loads[2].wait()
    xf = x_ref[...].astype(F32)
    xw[...] = (xf * wide_x).astype(BF16)
    e_copies = [send(xw, xw_far, e_sem_s.at[0], e_sem_r.at[0], mate)]
    loads[3].wait()
    gs[...] = (g_ref[...].astype(F32) * wide_g).astype(BF16)
    e_copies.append(send(gs, gs_far, e_sem_s.at[1], e_sem_r.at[1], mate))

    bc = mm(x_ref[:, own], w_ref[...])
    w_copy.wait()
    bc = (bc + mm(x_ref[:, far], w_other[...])).astype(BF16)
    b_in = bc[:, :state]
    c_out = bc[:, state:]

    bt[:, :rows] = jnp.concatenate([flip(b_in), flip(c_out)], axis=0)
    e_copies.append(send(bt.at[:, slice(0, rows)], bt.at[:, slice(rows, 2 * rows)],
                         e_sem_s.at[2], e_sem_r.at[2], mate))
    xs[...] = (x_ref[...].astype(F32) * gx[...]).astype(BF16)

    twice = jnp.where(ti == si, 2.0, 1.0).astype(F32)
    dots = mm(b_in, c_out, NT) * (twice * inv_root)
    upper = si >= ti
    lane = lax.broadcasted_iota(jnp.int32, (rows, 2 * head_dim), 1)

    def apart(cols):
        gp = g_ref[:, cols]
        zero = jnp.zeros_like(gp)
        return jnp.concatenate([jnp.where(lane < head_dim, gp, zero), jnp.where(lane < head_dim, zero, gp)], axis=0)

    wb = jnp.zeros((rows, rows), F32)
    for pair in range(head_count // 2):
        cols = slice(pair * 2 * head_dim, (pair + 1) * 2 * head_dim)
        cross = mm(xs[:, cols], apart(cols), NT)
        for j in range(2):
            h = 2 * pair + j
            gap = jnp.where(upper, incl_t[h:h + 1, :] - incl[:, h:h + 1], excl[:, h:h + 1] - excl_t[h:h + 1, :])
            mix = jnp.exp(gap)
            wb = wb + mix * cross[:, j * rows:(j + 1) * rows]
            pm[pair, :, j * rows:(j + 1) * rows] = (mix * dots).astype(BF16)
    wb = (wb * (twice * inv_root)).astype(BF16)
    e_copies[0].wait_recv()
    far_c = mm(xw_far[...], gs[...], NT).astype(BF16)
    e_copies[1].wait_recv()
    far_b = mm(xw[...], gs_far[...], NT).astype(BF16)
    e_copies[2].wait_recv()
    grad_b = mm(bt[state:, :], jnp.concatenate([wb, far_b], axis=1), NT)
    grad_c = mm(bt[:state, :], jnp.concatenate([wb, far_c], axis=0))
    grad_bc = jnp.concatenate([grad_b, grad_c], axis=0).astype(BF16)
    bc_all[0, :, band(ctx)] = grad_bc

    def b_copy(j, source, who):
        return remote(bc_all.at[0, :, band(source)], bc_all.at[j, :, band(source)],
                      b_sem_s.at[j], b_sem_r.at[j, source], who)

    b_copies = [b_copy(j, ctx, hubs[j - 1]) for j in far_first]
    for copy in b_copies:
        copy.start()
    mate_copies.append(b_copy(0, 0, mate))

    @pl.when(ctx == 0)
    def _():
        mate_copies[2].start()

    def finish_features():
        for pair in range(head_count // 2):
            cols = slice(pair * 2 * head_dim, (pair + 1) * 2 * head_dim)
            gx[:, cols] = gx[:, cols] * mm(pm[pair], apart(cols))
        gx[...] = mm(mm(b_in, bt[state:, rows:]).astype(BF16), gs_far[...]) * wide_x + gx[...]
        left = flip(grad_bc)
        gf_ref[:, own] = (gx[:, own] + mm(left, w_ref[...], NT)).astype(BF16)
        gf_ref[:, far] = (gx[:, far] + mm(left, w_other[...], NT)).astype(BF16)

    @pl.when(ctx == 0)
    def _():
        finish_features()

    scale = total_rows ** (-0.5)
    parts = 2
    h = 2 * state // parts
    parts_of = [slice(p * h, (p + 1) * h) for p in range(parts)]
    size = acc.shape[2]

    def gather_copy(j, t, p, k):
        return remote(full.at[j, :, parts_of[p]], gw_ref.at[place, lax.rem(t, per_shard), :, parts_of[p]],
                      ag_sem_s.at[j, k - 1, p], ag_sem_r.at[k - 1, lax.rem(t, per_shard), p],
                      {"dp": spot * QUAD + partner(place, k), "ctx": t // per_shard})

    def mate_copy(j, t, p):
        return remote(full.at[j, :, parts_of[p]], gw_ref.at[place, lax.rem(t, per_shard), :, parts_of[p]],
                      m_sem_s.at[j, p], m_sem_r.at[lax.rem(t, per_shard), p], mate)

    def spread_out(me, j, t, p):
        for k in far_first:
            gather_copy(j, t, p, k).start()

        @pl.when(t // per_shard != me)
        def _():
            mate_copy(j, t, p).start()

        @pl.when(t // per_shard == me)
        def _():
            gw_ref[place, lax.rem(t, per_shard), :, parts_of[p]] = full[j, :, parts_of[p]]

    def settle(me, j, t, p):
        for k in far_first:
            gather_copy(j, t, p, k).wait_send()

        @pl.when(t // per_shard != me)
        def _():
            mate_copy(j, t, p).wait_send()

    if line == blocks:
        owner = [partner(spot, j) for j in range(line)]
        handler = (1, 0, 1, 1)
    else:
        owner = [jnp.int32(t) for t in range(blocks)]
        handler = (1,) * blocks

    def along(j, p):
        return remote(full.at[0, :, parts_of[p]], full.at[j, :, parts_of[p]],
                      agz_sem_s.at[j - 1, p], agz_sem_r.at[j - 1, p], {**lines[j - 1], "ctx": handler[j]})

    def turned(v):
        return jnp.transpose(v * scale).astype(BF16)

    @pl.when(ctx == 1)
    def _():
        for copy in own_copies:
            copy.wait()
        for c in range(2):
            mate_copies[c].wait_recv()
        mate_copies[2].wait_recv()
        for j in far_first:
            for source in range(2):
                for c in range(2):
                    x_copy(j, c, source, hubs[j - 1]).wait_recv()
        total_t = [mm(bc_all[0], xr[0, c]) for c in range(2)]
        for j in far_first:
            for source in range(2):
                b_copy(j, source, hubs[j - 1]).wait_recv()
            total_t = [total_t[c] + mm(bc_all[j], xr[j, c]) for c in range(2)]
        for t in range(blocks):
            i = t % per_shard
            acc[t] = total_t[t // per_shard][:, i * size:(i + 1) * size]
            if line == blocks:
                z_send[t, 0] = acc[t].astype(BF16)

        if line == blocks:
            order = range(1, line)

            def z_copy(j, p):
                return remote(z_send.at[owner[j], 0, parts_of[p]], z_recv.at[j - 1, 0, parts_of[p]],
                              z_sem_s.at[j - 1, p], z_sem_r.at[j - 1, p], lines[j - 1])

            for p in range(parts):
                for j in reversed(order):
                    z_copy(j, p).start()
            finish_features()
            for p in range(parts):
                whole = acc[spot, parts_of[p]]
                for j in order:
                    z_copy(j, p).wait_recv()
                    whole = whole + z_recv[j - 1, 0, parts_of[p]].astype(F32)
                full[0, :, parts_of[p]] = turned(whole)
                for j in order:
                    along(j, p).start()
                spread_out(1, 0, spot, p)
            for p in range(parts):
                for j in order:
                    if handler[j] == 1:
                        along(j, p).wait_recv()
                        spread_out(1, j, owner[j], p)
            for p in range(parts):
                for j in order:
                    z_copy(j, p).wait_send()
                    along(j, p).wait_send()
        else:
            finish_features()
            for k in range(len(lines)):
                z_send[k] = acc[...].astype(BF16)
                copy = send(z_send.at[k], z_recv.at[k], z_sem_s.at[k, 0], z_sem_r.at[k, 0], lines[k])
                copy.wait()
                acc[...] = z_send[k].astype(F32) + z_recv[k].astype(F32)
            for t in range(blocks):
                for p in range(parts):
                    full[t, :, parts_of[p]] = turned(acc[t, parts_of[p]])
                    spread_out(1, t, owner[t], p)
        for j in range(blocks):
            for p in range(parts):
                if handler[j] == 1:
                    settle(1, j, owner[j], p)
                else:
                    @pl.when(owner[j] // per_shard == 1)
                    def _():
                        mate_copy(j, owner[j], p).wait_recv()

    @pl.when(ctx == 0)
    def _():
        for p in range(parts):
            for j in range(blocks):
                if handler[j] == 0:
                    along(j, p).wait_recv()
                    spread_out(0, j, owner[j], p)
        for j in range(blocks):
            for p in range(parts):
                if handler[j] == 0:
                    settle(0, j, owner[j], p)
                else:
                    @pl.when(owner[j] // per_shard == 0)
                    def _():
                        mate_copy(j, owner[j], p).wait_recv()

    for k in far_first:
        for i in range(per_shard):
            for p in range(parts):
                gather_copy(0, i, p, k).wait_recv()
    for copy in x_copies + b_copies + e_copies:
        copy.wait_send()

    @pl.when(ctx == 0)
    def _():
        for copy in mate_copies:
            copy.wait_send()


def deliver(gf_ref, gw_ref, gf_hbm, gw_hbm, sem):
    copies = [pltpu.make_async_copy(a, b, sem.at[k]) for k, (a, b) in enumerate(((gf_ref, gf_hbm), (gw_ref, gw_hbm)))]
    for copy in copies:
        copy.start()
    for copy in copies:
        copy.wait()


def per_device(dp_count, ctx_count, features, log_decays, cotangent, bc_weight):
    x, lr, g = features[0], jnp.swapaxes(log_decays[0], 0, 1), cotangent[0]
    rows, width = x.shape
    shard, cols = bc_weight.shape
    total_rows = features.shape[0] * dp_count * rows * ctx_count
    head_count = lr.shape[0]
    line = dp_count // QUAD
    quarter = shard // QUAD
    size = 128
    blocks = 2 * quarter // size
    direct = line == blocks
    hops = max(line - 1 if direct else line.bit_length() - 1, 1)
    deep = 1 if direct else blocks
    dma = pltpu.SemaphoreType.DMA
    vm = pl.BlockSpec(memory_space=pltpu.VMEM)
    gf, gw = pl.pallas_call(
        functools.partial(body, line, total_rows, head_count),
        out_shape=(pltpu.VMEM((rows, width), BF16), pltpu.VMEM((QUAD, blocks // 2, size, cols), BF16)),
        in_specs=[pl.BlockSpec(memory_space=pltpu.HBM)] * 4,
        out_specs=(vm, vm),
        scratch_shapes=[
            pltpu.VMEM((rows, width), BF16),
            pltpu.VMEM((head_count, rows), F32),
            pltpu.VMEM((rows, width), BF16),
            pltpu.VMEM((shard, cols), BF16),
            pltpu.VMEM((shard, cols), BF16),
            pltpu.VMEM((QUAD, 2, 2 * rows, quarter), BF16),
            pltpu.VMEM((rows, width), BF16),
            pltpu.VMEM((rows, width), BF16),
            pltpu.VMEM((rows, width), BF16),
            pltpu.VMEM((rows, width), BF16),
            pltpu.VMEM((rows, width), BF16),
            pltpu.VMEM((cols, 2 * rows), BF16),
            pltpu.VMEM((rows, width), F32),
            pltpu.VMEM((QUAD, cols, 2 * rows), BF16),
            pltpu.VMEM((head_count // 2, rows, 2 * rows), BF16),
            pltpu.VMEM((blocks, cols, size), F32),
            pltpu.VMEM((blocks if direct else hops, deep, cols, size), BF16),
            pltpu.VMEM((hops, deep, cols, size), BF16),
            pltpu.VMEM((blocks, size, cols), BF16),
            dma((4,)), dma((2,)), dma((3,)), dma((3,)),
            dma((QUAD, 2)), dma((QUAD, 2, 2)), dma((2,)), dma((QUAD,)), dma((QUAD, 2)),
            dma((hops, 2)), dma((hops, 2)), dma((hops, 2)), dma((hops, 2)),
            dma((blocks, QUAD - 1, 2)), dma((QUAD - 1, blocks // 2, 2)), dma((blocks, 2)), dma((blocks // 2, 2)),
        ],
        compiler_params=pltpu.CompilerParams(
            collective_id=0, has_side_effects=True, vmem_limit_bytes=64256 * 1024),
    )(x, lr, g, bc_weight)
    gw = gw.reshape(shard, cols)
    hbm = pl.BlockSpec(memory_space=pltpu.HBM)
    gf, gw = pl.pallas_call(
        deliver,
        out_shape=(jax.ShapeDtypeStruct((rows, width), BF16), jax.ShapeDtypeStruct((shard, cols), BF16)),
        in_specs=[vm, vm],
        out_specs=(hbm, hbm),
        scratch_shapes=[dma((2,))],
        compiler_params=pltpu.CompilerParams(vmem_limit_bytes=2 * 2**20),
    )(gf, gw)
    return gf[None], gw


def solution(mesh):
    placed = (P("dp", "ctx", None), P("dp", "ctx", None), P("dp", "ctx", None), P("ctx", None))
    return jax.shard_map(
        functools.partial(per_device, mesh.shape["dp"], mesh.shape["ctx"]),
        mesh=mesh,
        in_specs=placed,
        out_specs=(P("dp", "ctx", None), P("ctx", None)),
        check_vma=False,
    )
```

```python
import functools

import jax
import jax.numpy as jnp
from jax import lax
from jax.experimental import pallas as pl
from jax.experimental.pallas import tpu as pltpu
from jax.sharding import PartitionSpec as P

MESH = pl.DeviceIdType.MESH
F32 = jnp.float32
BF16 = jnp.bfloat16
NN = (((1,), (0,)), ((), ()))
NT = (((1,), (1,)), ((), ()))
QUAD = 4


def mm(a, b, dims=NN):
    return lax.dot_general(a, b, dims, preferred_element_type=F32)


def flip(a):
    return jnp.transpose(a.astype(F32)).astype(a.dtype)


def one_minus_exp(y):
    z = y * 0.125
    f = z * (1.0 + z * (1 / 2) * (1.0 + z * (1 / 3) * (1.0 + z * (1 / 4) * (1.0 + z * (1 / 5) * (1.0 + z * (1 / 6) * (1.0 + z * (1 / 7)))))))
    for _ in range(3):
        f = f * (f + 2.0)
    return -f


def partner(place, j):
    out, bit = place, 1
    while bit <= j:
        if j & bit:
            out = out + bit - 2 * bit * lax.rem(place // bit, 2)
        bit *= 2
    return out


def body(line, total_rows, head_count, x_hbm, lr_hbm, g_hbm, w_hbm, gf_ref, gw_ref,
         x_ref, lr_ref, g_ref, w_ref, w_other, xr, xs, xw, gs, xw_far, gs_far, bt, gx, bc_all,
         pm, acc, z_send, z_recv, full,
         in_sem, w_sem, e_sem_s, e_sem_r, x_sem_s, x_sem_r, o_sem, b_sem_s, b_sem_r,
         z_sem_s, z_sem_r, agz_sem_s, agz_sem_r, ag_sem_s, ag_sem_r, m_sem_s, m_sem_r):
    rows, width = x_ref.shape
    shard = w_ref.shape[0]
    state = w_ref.shape[1] // 2
    inv_root = state ** (-0.5)
    dp = lax.axis_index("dp")
    ctx = lax.axis_index("ctx")
    place = lax.rem(dp, QUAD)
    spot = dp // QUAD
    blocks = acc.shape[0]
    per_shard = blocks // 2
    mate = {"ctx": 1 - ctx}
    far_first = (3, 2, 1)
    hubs = [{"dp": spot * QUAD + partner(place, j), "ctx": 1} for j in range(1, QUAD)]
    leaves = [{"dp": spot * QUAD + partner(place, j), "ctx": 0} for j in range(1, QUAD)]
    if line == blocks:
        lines = [{"dp": partner(spot, j) * QUAD + place} for j in range(1, line)]
    else:
        lines = []
        m = 1
        while m < line:
            lines.append({"dp": dp + QUAD * m * (1 - 2 * lax.rem(spot // m, 2))})
            m *= 2

    def remote(src, dst, s_sem, r_sem, who):
        return pltpu.make_async_remote_copy(
            src_ref=src, dst_ref=dst, send_sem=s_sem, recv_sem=r_sem, device_id=who, device_id_type=MESH)

    def send(src, dst, s_sem, r_sem, who):
        copy = remote(src, dst, s_sem, r_sem, who)
        copy.start()
        return copy

    barrier = pltpu.get_barrier_semaphore()

    @pl.when(ctx == 1)
    def _():
        for who in hubs[::-1] + lines[::-1] + leaves:
            pl.semaphore_signal(barrier, inc=1, device_id=who, device_id_type=MESH)

    pl.semaphore_signal(barrier, inc=1, device_id=mate, device_id_type=MESH)

    loads = [pltpu.make_async_copy(a, b, in_sem.at[k])
             for k, (a, b) in enumerate(((x_hbm, x_ref), (lr_hbm, lr_ref), (w_hbm, w_ref), (g_hbm, g_ref)))]
    for load in loads:
        load.start()

    own = pl.ds(pl.multiple_of(ctx * shard, shard), shard)
    far = pl.ds(pl.multiple_of((1 - ctx) * shard, shard), shard)

    quarter = shard // QUAD

    def columns(c, q):
        return pl.ds(pl.multiple_of(c * shard + q * quarter, quarter), quarter)

    def band(k):
        return pl.ds(pl.multiple_of(k * rows, rows), rows)

    pl.semaphore_wait(barrier, QUAD + ctx * len(lines))
    w_copy = send(w_hbm, w_other, w_sem.at[0], w_sem.at[1], mate)

    def x_copy(j, c, source, who):
        return remote(x_ref.at[:, columns(c, partner(place, j))], xr.at[j, c, band(source)],
                      x_sem_s.at[j, c], x_sem_r.at[j, source, c], who)

    loads[0].wait()
    x_copies = [x_copy(j, c, ctx, hubs[j - 1]) for j, c in ((3, 0), (3, 1), (1, 0), (2, 0), (1, 1), (2, 1))]
    for copy in x_copies:
        copy.start()
    own_copies = [pltpu.make_async_copy(x_ref.at[:, columns(c, place)], xr.at[0, c, band(ctx)], o_sem.at[c])
                  for c in range(2)]
    mate_copies = [x_copy(0, c, 0, mate) for c in range(2)]

    @pl.when(ctx == 1)
    def _():
        for copy in own_copies:
            copy.start()

    @pl.when(ctx == 0)
    def _():
        for copy in mate_copies:
            copy.start()

    ti = lax.broadcasted_iota(jnp.int32, (rows, rows), 0)
    si = lax.broadcasted_iota(jnp.int32, (rows, rows), 1)
    tri = jnp.where(ti <= si, 1.0, 0.0).astype(F32)
    hi_ = lax.broadcasted_iota(jnp.int32, (rows, width), 0)
    ci_ = lax.broadcasted_iota(jnp.int32, (rows, width), 1)
    head_dim = width // head_count
    lo_c = hi_ * head_dim
    spread = jnp.where((ci_ >= lo_c) & (ci_ < lo_c + head_dim), 1.0, 0.0).astype(BF16)

    loads[1].wait()
    lr = lr_ref[...]
    lr_t = jnp.concatenate([lr, jnp.zeros((rows - head_count, rows), F32)], axis=0)
    incl_t = lax.dot_general(lr_t, tri, NN, precision=lax.Precision.HIGHEST, preferred_element_type=F32)
    excl_t = incl_t - lr_t
    lr_pad = jnp.transpose(lr_t)
    incl = jnp.transpose(incl_t)
    excl = incl - lr_pad
    total = incl[rows - 1:rows, :]
    step = jnp.sqrt(one_minus_exp(2.0 * lr_pad))
    first = ctx == 0
    rate_x = jnp.exp(jnp.where(first, total - incl, excl))
    rate_g = jnp.exp(jnp.where(first, total - excl, incl)) * inv_root

    twofold = jnp.concatenate([spread, spread], axis=0)

    def widen(v):
        top = v.astype(BF16)
        low = (v - top.astype(F32)).astype(BF16)
        return mm(jnp.concatenate([top, low], axis=1), twofold)

    wide = widen(jnp.concatenate([step, rate_x * step, rate_g], axis=0))
    step_w, wide_x, wide_g = (wide[k * rows:(k + 1) * rows] for k in range(3))
    gx[...] = step_w
    loads[2].wait()
    xf = x_ref[...].astype(F32)
    xw[...] = (xf * wide_x).astype(BF16)
    e_copies = [send(xw, xw_far, e_sem_s.at[0], e_sem_r.at[0], mate)]
    loads[3].wait()
    gs[...] = (g_ref[...].astype(F32) * wide_g).astype(BF16)
    e_copies.append(send(gs, gs_far, e_sem_s.at[1], e_sem_r.at[1], mate))

    bc = mm(x_ref[:, own], w_ref[...])
    w_copy.wait()
    bc = (bc + mm(x_ref[:, far], w_other[...])).astype(BF16)
    b_in = bc[:, :state]
    c_out = bc[:, state:]

    bt[:, :rows] = jnp.concatenate([flip(b_in), flip(c_out)], axis=0)
    e_copies.append(send(bt.at[:, slice(0, rows)], bt.at[:, slice(rows, 2 * rows)],
                         e_sem_s.at[2], e_sem_r.at[2], mate))
    xs[...] = (x_ref[...].astype(F32) * gx[...]).astype(BF16)

    twice = jnp.where(ti == si, 2.0, 1.0).astype(F32)
    dots = mm(b_in, c_out, NT) * (twice * inv_root)
    upper = si >= ti
    lane = lax.broadcasted_iota(jnp.int32, (rows, 2 * head_dim), 1)

    def apart(cols):
        gp = g_ref[:, cols]
        zero = jnp.zeros_like(gp)
        return jnp.concatenate([jnp.where(lane < head_dim, gp, zero), jnp.where(lane < head_dim, zero, gp)], axis=0)

    wb = jnp.zeros((rows, rows), F32)
    for pair in range(head_count // 2):
        cols = slice(pair * 2 * head_dim, (pair + 1) * 2 * head_dim)
        cross = mm(xs[:, cols], apart(cols), NT)
        for j in range(2):
            h = 2 * pair + j
            gap = jnp.where(upper, incl_t[h:h + 1, :] - incl[:, h:h + 1], excl[:, h:h + 1] - excl_t[h:h + 1, :])
            mix = jnp.exp(gap)
            wb = wb + mix * cross[:, j * rows:(j + 1) * rows]
            pm[pair, :, j * rows:(j + 1) * rows] = (mix * dots).astype(BF16)
    wb = (wb * (twice * inv_root)).astype(BF16)
    e_copies[0].wait_recv()
    far_c = mm(xw_far[...], gs[...], NT).astype(BF16)
    e_copies[1].wait_recv()
    far_b = mm(xw[...], gs_far[...], NT).astype(BF16)
    e_copies[2].wait_recv()
    grad_b = mm(bt[state:, :], jnp.concatenate([wb, far_b], axis=1), NT)
    grad_c = mm(bt[:state, :], jnp.concatenate([wb, far_c], axis=0))
    grad_bc = jnp.concatenate([grad_b, grad_c], axis=0).astype(BF16)
    bc_all[0, :, band(ctx)] = grad_bc

    def b_copy(j, source, who):
        return remote(bc_all.at[0, :, band(source)], bc_all.at[j, :, band(source)],
                      b_sem_s.at[j], b_sem_r.at[j, source], who)

    b_copies = [b_copy(j, ctx, hubs[j - 1]) for j in far_first]
    for copy in b_copies:
        copy.start()
    mate_copies.append(b_copy(0, 0, mate))

    @pl.when(ctx == 0)
    def _():
        mate_copies[2].start()

    def finish_features():
        for pair in range(head_count // 2):
            cols = slice(pair * 2 * head_dim, (pair + 1) * 2 * head_dim)
            gx[:, cols] = gx[:, cols] * mm(pm[pair], apart(cols))
        gx[...] = mm(mm(b_in, bt[state:, rows:]).astype(BF16), gs_far[...]) * wide_x + gx[...]
        left = flip(grad_bc)
        gf_ref[:, own] = (gx[:, own] + mm(left, w_ref[...], NT)).astype(BF16)
        gf_ref[:, far] = (gx[:, far] + mm(left, w_other[...], NT)).astype(BF16)

    @pl.when(ctx == 0)
    def _():
        finish_features()

    scale = total_rows ** (-0.5)
    parts = 2
    h = 2 * state // parts
    parts_of = [slice(p * h, (p + 1) * h) for p in range(parts)]
    size = acc.shape[2]

    def gather_copy(j, t, p, k):
        return remote(full.at[j, :, parts_of[p]], gw_ref.at[place, lax.rem(t, per_shard), :, parts_of[p]],
                      ag_sem_s.at[j, k - 1, p], ag_sem_r.at[k - 1, lax.rem(t, per_shard), p],
                      {"dp": spot * QUAD + partner(place, k), "ctx": t // per_shard})

    def mate_copy(j, t, p):
        return remote(full.at[j, :, parts_of[p]], gw_ref.at[place, lax.rem(t, per_shard), :, parts_of[p]],
                      m_sem_s.at[j, p], m_sem_r.at[lax.rem(t, per_shard), p], mate)

    def spread_out(me, j, t, p):
        for k in far_first:
            gather_copy(j, t, p, k).start()

        @pl.when(t // per_shard != me)
        def _():
            mate_copy(j, t, p).start()

        @pl.when(t // per_shard == me)
        def _():
            gw_ref[place, lax.rem(t, per_shard), :, parts_of[p]] = full[j, :, parts_of[p]]

    def settle(me, j, t, p):
        for k in far_first:
            gather_copy(j, t, p, k).wait_send()

        @pl.when(t // per_shard != me)
        def _():
            mate_copy(j, t, p).wait_send()

    if line == blocks:
        owner = [partner(spot, j) for j in range(line)]
        handler = (1, 0, 1, 1)
    else:
        owner = [jnp.int32(t) for t in range(blocks)]
        handler = (1,) * blocks

    def along(j, p):
        return remote(full.at[0, :, parts_of[p]], full.at[j, :, parts_of[p]],
                      agz_sem_s.at[j - 1, p], agz_sem_r.at[j - 1, p], {**lines[j - 1], "ctx": handler[j]})

    def turned(v):
        return jnp.transpose(v * scale).astype(BF16)

    @pl.when(ctx == 1)
    def _():
        for copy in own_copies:
            copy.wait()
        for c in range(2):
            mate_copies[c].wait_recv()
        mate_copies[2].wait_recv()
        for j in far_first:
            for source in range(2):
                for c in range(2):
                    x_copy(j, c, source, hubs[j - 1]).wait_recv()
        total_t = [mm(bc_all[0], xr[0, c]) for c in range(2)]
        for j in far_first:
            for source in range(2):
                b_copy(j, source, hubs[j - 1]).wait_recv()
            total_t = [total_t[c] + mm(bc_all[j], xr[j, c]) for c in range(2)]
        for t in range(blocks):
            i = t % per_shard
            acc[t] = total_t[t // per_shard][:, i * size:(i + 1) * size]
            if line == blocks:
                z_send[t, 0] = acc[t].astype(BF16)

        if line == blocks:
            order = range(1, line)

            def z_copy(j, p):
                return remote(z_send.at[owner[j], 0, parts_of[p]], z_recv.at[j - 1, 0, parts_of[p]],
                              z_sem_s.at[j - 1, p], z_sem_r.at[j - 1, p], lines[j - 1])

            for p in range(parts):
                for j in reversed(order):
                    z_copy(j, p).start()
            finish_features()
            for p in range(parts):
                whole = acc[spot, parts_of[p]]
                for j in order:
                    z_copy(j, p).wait_recv()
                    whole = whole + z_recv[j - 1, 0, parts_of[p]].astype(F32)
                full[0, :, parts_of[p]] = turned(whole)
                for j in order:
                    along(j, p).start()
                spread_out(1, 0, spot, p)
            for p in range(parts):
                for j in order:
                    if handler[j] == 1:
                        along(j, p).wait_recv()
                        spread_out(1, j, owner[j], p)
            for p in range(parts):
                for j in order:
                    z_copy(j, p).wait_send()
                    along(j, p).wait_send()
        else:
            finish_features()
            for k in range(len(lines)):
                z_send[k] = acc[...].astype(BF16)
                copy = send(z_send.at[k], z_recv.at[k], z_sem_s.at[k, 0], z_sem_r.at[k, 0], lines[k])
                copy.wait()
                acc[...] = z_send[k].astype(F32) + z_recv[k].astype(F32)
            for t in range(blocks):
                for p in range(parts):
                    full[t, :, parts_of[p]] = turned(acc[t, parts_of[p]])
                    spread_out(1, t, owner[t], p)
        for j in range(blocks):
            for p in range(parts):
                if handler[j] == 1:
                    settle(1, j, owner[j], p)
                else:
                    @pl.when(owner[j] // per_shard == 1)
                    def _():
                        mate_copy(j, owner[j], p).wait_recv()

    @pl.when(ctx == 0)
    def _():
        for p in range(parts):
            for j in range(blocks):
                if handler[j] == 0:
                    along(j, p).wait_recv()
                    spread_out(0, j, owner[j], p)
        for j in range(blocks):
            for p in range(parts):
                if handler[j] == 0:
                    settle(0, j, owner[j], p)
                else:
                    @pl.when(owner[j] // per_shard == 0)
                    def _():
                        mate_copy(j, owner[j], p).wait_recv()

    for k in far_first:
        for i in range(per_shard):
            for p in range(parts):
                gather_copy(0, i, p, k).wait_recv()
    for copy in x_copies + b_copies + e_copies:
        copy.wait_send()

    @pl.when(ctx == 0)
    def _():
        for copy in mate_copies:
            copy.wait_send()


def deliver(gf_ref, gw_ref, gf_hbm, gw_hbm, sem):
    copies = [pltpu.make_async_copy(a, b, sem.at[k]) for k, (a, b) in enumerate(((gf_ref, gf_hbm), (gw_ref, gw_hbm)))]
    for copy in copies:
        copy.start()
    for copy in copies:
        copy.wait()


def per_device(dp_count, ctx_count, features, log_decays, cotangent, bc_weight):
    x, lr, g = features[0], jnp.swapaxes(log_decays[0], 0, 1), cotangent[0]
    rows, width = x.shape
    shard, cols = bc_weight.shape
    total_rows = features.shape[0] * dp_count * rows * ctx_count
    head_count = lr.shape[0]
    line = dp_count // QUAD
    quarter = shard // QUAD
    size = 128
    blocks = 2 * quarter // size
    direct = line == blocks
    hops = max(line - 1 if direct else line.bit_length() - 1, 1)
    deep = 1 if direct else blocks
    dma = pltpu.SemaphoreType.DMA
    vm = pl.BlockSpec(memory_space=pltpu.VMEM)
    gf, gw = pl.pallas_call(
        functools.partial(body, line, total_rows, head_count),
        out_shape=(pltpu.VMEM((rows, width), BF16), pltpu.VMEM((QUAD, blocks // 2, size, cols), BF16)),
        in_specs=[pl.BlockSpec(memory_space=pltpu.HBM)] * 4,
        out_specs=(vm, vm),
        scratch_shapes=[
            pltpu.VMEM((rows, width), BF16),
            pltpu.VMEM((head_count, rows), F32),
            pltpu.VMEM((rows, width), BF16),
            pltpu.VMEM((shard, cols), BF16),
            pltpu.VMEM((shard, cols), BF16),
            pltpu.VMEM((QUAD, 2, 2 * rows, quarter), BF16),
            pltpu.VMEM((rows, width), BF16),
            pltpu.VMEM((rows, width), BF16),
            pltpu.VMEM((rows, width), BF16),
            pltpu.VMEM((rows, width), BF16),
            pltpu.VMEM((rows, width), BF16),
            pltpu.VMEM((cols, 2 * rows), BF16),
            pltpu.VMEM((rows, width), F32),
            pltpu.VMEM((QUAD, cols, 2 * rows), BF16),
            pltpu.VMEM((head_count // 2, rows, 2 * rows), BF16),
            pltpu.VMEM((blocks, cols, size), F32),
            pltpu.VMEM((blocks if direct else hops, deep, cols, size), BF16),
            pltpu.VMEM((hops, deep, cols, size), BF16),
            pltpu.VMEM((blocks, size, cols), BF16),
            dma((4,)), dma((2,)), dma((3,)), dma((3,)),
            dma((QUAD, 2)), dma((QUAD, 2, 2)), dma((2,)), dma((QUAD,)), dma((QUAD, 2)),
            dma((hops, 2)), dma((hops, 2)), dma((hops, 2)), dma((hops, 2)),
            dma((blocks, QUAD - 1, 2)), dma((QUAD - 1, blocks // 2, 2)), dma((blocks, 2)), dma((blocks // 2, 2)),
        ],
        compiler_params=pltpu.CompilerParams(
            collective_id=0, has_side_effects=True, vmem_limit_bytes=64256 * 1024),
    )(x, lr, g, bc_weight)
    gw = gw.reshape(shard, cols)
    hbm = pl.BlockSpec(memory_space=pltpu.HBM)
    gf, gw = pl.pallas_call(
        deliver,
        out_shape=(jax.ShapeDtypeStruct((rows, width), BF16), jax.ShapeDtypeStruct((shard, cols), BF16)),
        in_specs=[vm, vm],
        out_specs=(hbm, hbm),
        scratch_shapes=[dma((2,))],
        compiler_params=pltpu.CompilerParams(vmem_limit_bytes=2 * 2**20),
    )(gf, gw)
    return gf[None], gw


def solution(mesh):
    placed = (P("dp", "ctx", None), P("dp", "ctx", None), P("dp", "ctx", None), P("ctx", None))
    return jax.shard_map(
        functools.partial(per_device, mesh.shape["dp"], mesh.shape["ctx"]),
        mesh=mesh,
        in_specs=placed,
        out_specs=(P("dp", "ctx", None), P("ctx", None)),
        check_vma=False,
    )
```
